32 devices in a mesh: ops: 16 (over z, x, core), sec: 2 (over y).
Axes of the slice: x: 2, y: 2, z: 4, core: 2. Of those that a mesh axis runs over, the one named last changes fastest.
Arguments:
- wavefunction: bfloat16 [8, 512, 512], P('sec'), may hold values from -6 to 6
- left_ops: bfloat16 [16, 512, 512], P('ops'), may hold values from -0.25 to 0.25
- right_ops: bfloat16 [16, 512, 512], P('ops'), may hold values from -0.25 to 0.25
- shift_map: int32 [16], P('ops'), may hold values from 0 to 7
- sector_sizes: int32 [8], replicated, may hold values from 256 to 512, as said below
- step_sizes: int32 [2], replicated, may hold values from 1 to 5
- integrals: float32 [16, 3], P('ops'), may hold values from 0.25 to 1
Outputs:
- final_wave: float32 [8, 512, 512], P('sec')
- mixed_ops: bfloat16 [16, 512, 512], P('ops', None, 'sec')
The draws below stay inside these ranges and needn't reach their ends.
Inputs may be any that keep to these rules, and one draw needn't show every extreme that they name: `sector_sizes`: each sector holds between 256 and 512 states; some sector holds exactly 512.
All inputs are finite; a program needn't handle non-finite values.
Results may differ from the reference program's by a relative error of at most 0.015.
Values may be sent and summed in bfloat16 or wider, within the bound.
No kernel may reach another device: no remote copies, remote signals or barrier semaphores. Data moves between devices by JAX's collectives and lax.ppermute only.
A program may use at most 64 MiB of HBM per device.

```python
import jax
import jax.numpy as jnp
from jax import lax

M = 512
S = 8
ITERS = 2
OPERATORS = 16


def draw_sector_sizes(key, part):
    first_key = jax.random.fold_in(key, 11)
    second_key = jax.random.fold_in(key, 23)
    sizes = jax.random.randint(first_key, (S,), M // 2, M + 1).astype(jnp.int32)
    chosen = jax.random.randint(second_key, (), 0, S).astype(jnp.int32)
    return jnp.where(jnp.arange(S, dtype=jnp.int32) == chosen, M, sizes).astype(jnp.int32)


def plant(entries, rng, least, high):
    dims = entries.shape
    place = [jax.random.randint(jax.random.fold_in(rng, axis), (), 0, dims[axis]) for axis in range(len(dims))]
    entries = entries.at[tuple(place)].set(least)
    longest = dims.index(max(dims))
    place[longest] = (place[longest] + 1) % dims[longest]
    return entries.at[tuple(place)].set(high)


def block_scale(key, dims, split, low, largest):
    gain = 1.0
    for axis_at, blocks in split:
        draws = jax.random.uniform(jax.random.fold_in(jax.random.fold_in(key, 6), axis_at), (blocks,), jnp.float32, low / len(split), largest / len(split))
        gain = gain * jnp.repeat(jnp.exp(draws), dims[axis_at] // blocks).reshape((-1,) + (1,) * (len(dims) - 1 - axis_at))
    return gain


def normal_values(key, extent, scale, bound, pieces=(), kind=jnp.bfloat16):
    level = block_scale(key, extent, pieces, -0.22, 0.18) if pieces else 1.0
    entries = jax.random.normal(key, extent, jnp.float32) * scale * level
    return jnp.minimum(jnp.maximum(entries, -bound), bound).astype(kind)


def setup_inputs(seed: int = 0) -> dict:
    key_list = jax.random.split(jax.random.key(seed), 8)
    wavefunction = normal_values(key_list[0], (S, M, M), 1.0, 6.0, ((0, 2),))
    left_ops = normal_values(key_list[1], (OPERATORS, M, M), M ** -0.5, 0.25, ((0, 16),))
    right_ops = normal_values(key_list[2], (OPERATORS, M, M), M ** -0.5, 0.25, ((0, 16),))
    shift_map = plant(jax.random.randint(key_list[3], (OPERATORS,), 0, S), jax.random.fold_in(key_list[3], 1), 0, S - 1).astype(jnp.int32)
    sector_sizes = draw_sector_sizes(jax.random.fold_in(key_list[7], 71), 0)
    step_sizes = jax.random.randint(key_list[5], (ITERS,), 1, 6).astype(jnp.int32)
    integrals = jnp.clip(0.25 + 0.75 * jax.random.uniform(key_list[6], (OPERATORS, 3), jnp.float32) ** block_scale(key_list[6], (OPERATORS, 3), ((0, 16),), -0.2, 0.2), 0.25, 1.0)
    return {"wavefunction": wavefunction, "left_ops": left_ops, "right_ops": right_ops, "shift_map": shift_map, "sector_sizes": sector_sizes, "step_sizes": step_sizes, "integrals": integrals}


def reference(wavefunction, left_ops, right_ops, shift_map, sector_sizes, step_sizes, integrals):
    highest = lax.Precision.HIGHEST
    sectors = wavefunction.shape[0]
    width = wavefunction.shape[1]
    count = left_ops.shape[0]
    column = jnp.arange(width, dtype=jnp.int32)
    row_ok = (column[None, :] < sector_sizes[:, None]).astype(jnp.float32)
    mask = row_ok[:, :, None] * row_ok[:, None, :]
    psi = wavefunction.astype(jnp.float32) * mask
    order = jnp.arange(sectors, dtype=jnp.int32)

    def apply(state):
        state_low = state.astype(jnp.bfloat16).astype(jnp.float32)

        def one(total, member):
            left, right, shift = member
            source = jnp.take(state_low, ((order - shift) % sectors).astype(jnp.int32), axis=0)
            inner = jnp.einsum('mn,snp->smp', left.astype(jnp.float32), source, precision=highest)
            inner = inner.astype(jnp.bfloat16).astype(jnp.float32)
            return (total + jnp.einsum('smp,qp->smq', inner, right.astype(jnp.float32), precision=highest), None)
        total, _ = lax.scan(one, jnp.zeros_like(state), (left_ops, right_ops, shift_map))
        return total
    for step in range(ITERS):
        hpsi = apply(psi)
        factor = step_sizes[step].astype(jnp.float32) / (8.0 * jnp.sqrt(jnp.float32(count)))
        psi = mask * (psi - factor * hpsi)
        total = jnp.sum(psi * psi)
        psi = psi / jnp.sqrt(total / (sectors * width * width) + 1e-06)
    basis = psi[0].astype(jnp.bfloat16).astype(jnp.float32)

    def rotate(left):
        half = jnp.dot(basis.T, left.astype(jnp.float32), precision=highest)
        half = half.astype(jnp.bfloat16).astype(jnp.float32)
        return jnp.dot(half, basis, precision=highest) / width
    rotated = lax.map(rotate, left_ops)
    padded = jnp.pad(rotated, ((1, 1), (0, 0), (0, 0)))
    mixed = integrals[:, 0, None, None] * padded[:-2] + integrals[:, 1, None, None] * padded[1:-1] + integrals[:, 2, None, None] * padded[2:]
    return (psi, mixed.astype(jnp.bfloat16))
```

```python
import functools
import math

import jax
import jax.numpy as jnp
import numpy as np
from jax import lax
from jax.experimental import pallas as pl
from jax.experimental.pallas import tpu as pltpu
from jax.sharding import PartitionSpec as P

ITERS = 2
GATHER_BYTES = 8 * 1024 * 1024
VMEM = pltpu.MemorySpace.VMEM
SMEM = pltpu.MemorySpace.SMEM


def broadcast(value, axis, source):
    kept = jnp.where(lax.axis_index(axis) == source, value, 0).astype(value.dtype)
    return lax.psum(kept, axis)


def padded_2(cells, sides, width):
    for axis, dim in sides:
        count = lax.axis_size(axis)
        ends = count - 1
        head = lax.slice_in_dim(cells, 0, width, axis=dim)
        tail = lax.slice_in_dim(cells, cells.shape[dim] - width, cells.shape[dim], axis=dim)
        cells = jnp.concatenate(
            [
                lax.ppermute(tail, axis, [(i, (i + 1) % count) for i in range(ends)]),
                cells,
                lax.ppermute(head, axis, [((i + 1) % count, i) for i in range(ends)]),
            ],
            axis=dim,
        )
    return cells


def reduce_form(wavefunction, left_ops, right_ops, shift_map, sector_sizes, step_sizes, integrals):
    highest = lax.Precision.HIGHEST
    local_sec = wavefunction.shape[0]
    width = wavefunction.shape[1]
    sectors = sector_sizes.shape[0]
    count = lax.axis_size("ops") * left_ops.shape[0]
    first = lax.axis_index("sec") * local_sec
    local_sizes = lax.dynamic_slice_in_dim(sector_sizes, first, local_sec, 0)
    column = jnp.arange(width, dtype=jnp.int32)
    row_ok = (column[None, :] < local_sizes[:, None]).astype(jnp.float32)
    mask = row_ok[:, :, None] * row_ok[:, None, :]
    psi = wavefunction.astype(jnp.float32) * mask
    sources = first + jnp.arange(local_sec, dtype=jnp.int32)
    target = (sources[None, :] + shift_map[:, None]) % sectors
    routing = (jnp.arange(sectors, dtype=jnp.int32)[:, None, None] == target[None]).astype(
        jnp.float32
    )
    for step in range(ITERS):
        psi_low = psi.astype(jnp.bfloat16)
        inner = jnp.einsum(
            "kmn,snp->ksmp", left_ops, psi_low, preferred_element_type=jnp.float32
        ).astype(jnp.bfloat16)
        terms = jnp.einsum("ksmp,kqp->ksmq", inner, right_ops, preferred_element_type=jnp.float32)
        contrib = jnp.einsum("tks,ksmq->tmq", routing, terms, precision=highest)
        partial_rows = lax.psum_scatter(contrib, "ops", scatter_dimension=1, tiled=True)
        own_rows = lax.psum_scatter(
            partial_rows.astype(jnp.bfloat16), "sec", scatter_dimension=0, tiled=True
        ).astype(jnp.float32)
        hpsi = lax.all_gather(own_rows.astype(jnp.bfloat16), "ops", axis=1, tiled=True).astype(
            own_rows.dtype
        )
        factor = step_sizes[step].astype(jnp.float32) / (8.0 * math.sqrt(count))
        psi = mask * (psi - factor * hpsi)
        total = lax.psum(jnp.sum(psi * psi), "sec")
        psi = psi / jnp.sqrt(total / (sectors * width * width) + 1e-06)
    basis = broadcast(psi[0].astype(jnp.bfloat16), "sec", 0)
    col_count = width // lax.axis_size("sec")
    basis_cols = lax.dynamic_slice_in_dim(basis, lax.axis_index("sec") * col_count, col_count, 1)
    half = jnp.einsum("mp,kmn->kpn", basis, left_ops, preferred_element_type=jnp.float32).astype(
        jnp.bfloat16
    )
    rotated = (
        jnp.einsum("kpn,nq->kpq", half, basis_cols, preferred_element_type=jnp.float32) / width
    )
    padded = padded_2(rotated.astype(jnp.bfloat16), (("ops", 0),), 1).astype(rotated.dtype)
    mixed = (
        integrals[:, 0, None, None] * padded[:-2]
        + integrals[:, 1, None, None] * padded[1:-1]
        + integrals[:, 2, None, None] * padded[2:]
    )
    return (psi, mixed.astype(jnp.bfloat16))


def ring_order(chips):
    return list(range(0, chips, 2)) + list(range(chips - 1, 0, -2))


def swap_core(x, n):
    return lax.ppermute(x, "ops", [(o, o ^ 1) for o in range(n)])


def swap_sec(x):
    return lax.ppermute(x, "sec", [(0, 1), (1, 0)])


def along_ring(x, n, by):
    order = ring_order(n // 2)
    place = {chip: i for i, chip in enumerate(order)}
    perm = []
    for o in range(n):
        chip = order[(place[o // 2] + by) % len(order)]
        perm.append((o, 2 * chip + o % 2))
    return lax.ppermute(x, "ops", perm)


def ring_slots(n):
    chips = n // 2
    slots = [(0, 0, None)]
    for step in range(1, chips // 2):
        slots += [(-step, 0, None), (step, 0, None)]
    slots += [(chips // 2, 0, 0), (chips // 2, 0, 1)]
    return slots + [(d, 1, part) for d, _, part in slots]


def ring_table(n):
    order = ring_order(n // 2)
    place = {chip: i for i, chip in enumerate(order)}
    rows = []
    for o in range(n):
        at = place[o // 2]
        rows.append([2 * order[(at + d) % len(order)] + ((o % 2) ^ c) for d, c, _ in ring_slots(n)])
    return np.array(rows, np.int32)


def ring_gather(x, n):
    chips = n // 2
    half = x.shape[0] // 2
    up = down = x
    own = [x]
    for step in range(1, chips // 2):
        up, down = along_ring(up, n, 1), along_ring(down, n, -1)
        own += [up, down]
    own += [along_ring(up[:half], n, 1), along_ring(down[half:], n, -1)]
    return own + [swap_core(piece, n) for piece in own]


def copy_in(pairs, sems):
    copies = []
    for i, (src, dst) in enumerate(pairs):
        copy = pltpu.make_async_copy(src, dst, sems.at[i])
        copy.start()
        copies.append(copy)
    return copies


def place_inner(inner, left_ref, psi, shift_ref, sector, columns):
    count, sectors, rows, _ = inner.shape
    product = jnp.dot(left_ref[...], psi, preferred_element_type=jnp.float32).astype(jnp.bfloat16)
    for k in range(count):
        target = lax.rem(sector + shift_ref[k], sectors)
        inner[k, target, :, columns] = product[k * rows : (k + 1) * rows]


def first_kernel(scal_ref, shift_ref, sizes_ref, left_ref, own_ref, near_ref, far_ref, inner_ref):
    core, sec = scal_ref[1], scal_ref[2]
    local = own_ref.shape[0]
    width = own_ref.shape[1]
    for ref, base in (
        (own_ref, sec * local),
        (near_ref, (1 - sec) * local + core * (local // 2)),
        (far_ref, (1 - sec) * local + (1 - core) * (local // 2)),
    ):

        @pl.loop(0, ref.shape[0])
        def _(i):
            sector = base + i
            size = sizes_ref[sector]
            psi = ref[i]
            row = lax.broadcasted_iota(jnp.int32, psi.shape, 0)
            col = lax.broadcasted_iota(jnp.int32, psi.shape, 1)
            psi = jnp.where((row < size) & (col < size), psi, jnp.zeros_like(psi))
            place_inner(inner_ref, left_ref, psi, shift_ref, sector, slice(0, width))


def second_stage(inner, right, acc):
    count, sectors, rows, width = inner.shape
    acc[...] = jnp.zeros_like(acc)

    @pl.loop(0, count)
    def _(k):
        lhs = inner[k].reshape(sectors * rows, width)
        acc[...] += lax.dot_general(
            lhs, right[k], (((1,), (1,)), ((), ())), preferred_element_type=jnp.float32
        )


def step_rows(psi, acc, sizes_ref, scal_ref, factor, sector):
    rows, cols = psi.shape
    size = sizes_ref[sector]
    row = lax.broadcasted_iota(jnp.int32, psi.shape, 0) + scal_ref[0] * rows
    col = lax.broadcasted_iota(jnp.int32, psi.shape, 1) + scal_ref[2] * cols
    moved = psi - factor * acc[sector * rows : (sector + 1) * rows]
    return jnp.where((row < size) & (col < size), moved, 0.0)


def right_pairs(table_ref, pieces, right, slots):
    half = right.shape[1] // 2
    pairs = []
    for i, (piece, (_, _, part)) in enumerate(zip(pieces, slots)):
        k = table_ref[i]
        if part is None:
            pairs.append((piece, right.at[k]))
        else:
            pairs.append((piece, right.at[k, part * half : (part + 1) * half]))
    return pairs


def iter1_kernel(slots, *refs):
    n_slots = len(slots)
    scal_ref, table_ref, sizes_ref, factor_ref, inner, own_ref, near_ref, far_ref = refs[:8]
    pieces = refs[8 : 8 + n_slots]
    out_ref, send_ref, right, start, acc, sems = refs[8 + n_slots :]
    o, core, sec = scal_ref[0], scal_ref[1], scal_ref[2]
    local = own_ref.shape[0]
    _, rows, cols = out_ref.shape
    here = (pl.ds(o * rows, rows), pl.ds(sec * cols, cols))
    foreign = (1 - sec) * local
    pairs = right_pairs(table_ref, pieces, right, slots)
    pairs += [
        (own_ref.at[(slice(None),) + here], start.at[pl.ds(sec * local, local)]),
        (near_ref.at[(slice(None),) + here], start.at[pl.ds(foreign + core * (local // 2), local // 2)]),
        (far_ref.at[(slice(None),) + here], start.at[pl.ds(foreign + (1 - core) * (local // 2), local // 2)]),
    ]
    for copy in copy_in(pairs, sems):
        copy.wait()
    second_stage(inner, right, acc)
    for s in range(out_ref.shape[0]):
        moved = step_rows(start[s].astype(jnp.float32), acc, sizes_ref, scal_ref, factor_ref[0], s)
        out_ref[s] = moved
        send_ref[s] = moved.astype(jnp.bfloat16)


def split_3(value):
    parts = []
    for _ in range(3):
        low = value.astype(jnp.bfloat16)
        parts.append(low)
        value = value - low.astype(jnp.float32)
    return parts


def iter2_kernel(slots, *refs):
    n_slots = len(slots)
    scal_ref, table_ref, shift_ref, sizes_ref, factor_ref, left_ref, prev_ref = refs[:7]
    psi_pieces = refs[7 : 7 + n_slots]
    right_pieces = refs[7 + n_slots : 7 + 2 * n_slots]
    keep_ref, send_ref, psi, inner, right, acc, low, psems, rsems = refs[7 + 2 * n_slots :]
    sec = scal_ref[2]
    sectors, rows, cols = prev_ref.shape
    local = sectors // 2
    pairs = []
    for i, (piece, (_, _, part)) in enumerate(zip(psi_pieces, slots)):
        at = pl.ds(table_ref[i] * rows, rows)
        for h in range(2) if part is None else (part,):
            side = sec if h == 0 else 1 - sec
            pairs.append((piece.at[h if part is None else 0], psi.at[side, :, at]))
    psi_copies = copy_in(pairs, psems)
    right_copies = copy_in(right_pairs(table_ref, right_pieces, right, slots), rsems)
    for copy in psi_copies:
        copy.wait()

    @pl.loop(0, sectors)
    def _(s):
        for h in range(2):
            place_inner(inner, left_ref, psi[h, s], shift_ref, s, slice(h * cols, (h + 1) * cols))

    for copy in right_copies:
        copy.wait()
    second_stage(inner, right, acc)
    before = jnp.zeros((rows, cols), jnp.float32)
    after = jnp.zeros((rows, cols), jnp.float32)
    for s in range(sectors):
        old = prev_ref[s]
        moved = step_rows(old, acc, sizes_ref, scal_ref, factor_ref[0], s)
        low[s] = moved.astype(jnp.bfloat16)
        before += old * old
        after += moved * moved
    for i in range(local):
        keep_ref[i * rows : (i + 1) * rows] = low[sec * local + i]
        send_ref[i * rows : (i + 1) * rows] = low[(1 - sec) * local + i]
    keep_ref[local * rows : (local + 1) * rows] = low[0]
    send_ref[local * rows : (local + 1) * rows] = low[0]
    tail = keep_ref.shape[0] - (local + 1) * rows
    line = lax.broadcasted_iota(jnp.int32, (tail, cols), 0)
    stats = jnp.zeros((tail, cols), jnp.float32)
    for i, total in enumerate((before, after)):
        parts = split_3(jnp.full((tail, cols), jnp.sum(total), jnp.float32))
        for p, low_part in enumerate(parts):
            stats = jnp.where(line == 3 * i + p, low_part.astype(jnp.float32), stats)
    keep_ref[(local + 1) * rows :] = stats.astype(jnp.bfloat16)
    send_ref[(local + 1) * rows :] = stats.astype(jnp.bfloat16)


def final_kernel(slots, values, *refs):
    n_slots = len(slots)
    scal_ref, table_ref, mixer_ref = refs[:3]
    pieces = refs[3 : 3 + n_slots]
    wave_ref, mixed_ref, basis, sems = refs[3 + n_slots :]
    sec = scal_ref[2]
    local, width, _ = wave_ref.shape
    cols = width // 2
    n = n_slots - 2
    rows = width // n
    tail = pieces[0].shape[1] - (local + 1) * rows
    stats = jnp.zeros((tail, cols), jnp.float32)
    views = []
    for i, (piece, (_, _, part)) in enumerate(zip(pieces, slots)):
        at = pl.ds(pl.multiple_of(table_ref[i] * rows, rows), rows)
        for h in range(2) if part is None else (part,):
            side = sec if h == 0 else 1 - sec
            across = pl.ds(pl.multiple_of(side * cols, cols), cols)
            view = piece.at[h if part is None else 0]
            views.append((view, at, across))
            stats += view[(local + 1) * rows :].astype(jnp.float32)
            basis[at, across] = view[local * rows : (local + 1) * rows]
    line = lax.broadcasted_iota(jnp.int32, (tail, cols), 0)
    first = jnp.sum(jnp.where(line < 3, stats, 0.0), axis=0, keepdims=True)[:, :1]
    second = jnp.sum(jnp.where((line >= 3) & (line < 6), stats, 0.0), axis=0, keepdims=True)[:, :1]
    norm_1 = jnp.sqrt(first / values + 1e-06)
    norm_2 = jnp.sqrt(second / (norm_1 * norm_1) / values + 1e-06)
    scale = 1.0 / (norm_1 * norm_2)
    for s in range(local):
        for view, at, across in views:
            wave_ref[s, at, across] = view[s * rows : (s + 1) * rows].astype(jnp.float32) * scale
    across = pl.ds(pl.multiple_of(sec * cols, cols), cols)
    right = jnp.dot(mixer_ref[...], basis[:, across], preferred_element_type=jnp.float32)
    rotated = lax.dot_general(
        basis[...], right.astype(jnp.bfloat16), (((0,), (0,)), ((), ())), preferred_element_type=jnp.float32
    )
    mixed_ref[...] = (rotated * (scale * scale / width)).astype(jnp.bfloat16)


def gather_form(wavefunction, left_ops, right_ops, shift_map, sector_sizes, step_sizes, integrals):
    f32, bf16 = jnp.float32, jnp.bfloat16
    n = lax.axis_size("ops")
    local, width, _ = wavefunction.shape
    sectors = sector_sizes.shape[0]
    rows, cols = width // n, width // 2
    o, sec = lax.axis_index("ops"), lax.axis_index("sec")
    core = lax.rem(o, 2)
    slots = ring_slots(n)
    n_slots = len(slots)
    scal = jnp.stack([o, core, sec]).astype(jnp.int32)
    table = lax.dynamic_slice_in_dim(jnp.asarray(ring_table(n)), o, 1, 0)[0]
    factors = step_sizes.astype(f32) / (8.0 * math.sqrt(n))
    any_spec = pl.BlockSpec(memory_space=pl.ANY)
    vmem_spec = pl.BlockSpec(memory_space=VMEM)
    smem_spec = pl.BlockSpec(memory_space=SMEM)
    params = pltpu.CompilerParams(vmem_limit_bytes=56 * 1024 * 1024)

    right_cols = lax.dynamic_slice_in_dim(right_ops[0], sec * cols, cols, 0)
    part = lax.dynamic_slice_in_dim(wavefunction, core * (local // 2), local // 2, 0)
    near = swap_sec(part)
    far = swap_core(near, n)
    right_pieces = ring_gather(right_cols, n)
    shifts = lax.all_gather(shift_map, "ops", tiled=True)
    left_rows = lax.all_to_all(left_ops[0], "ops", 0, 0, tiled=True)

    inner = pl.pallas_call(
        first_kernel,
        out_shape=jax.ShapeDtypeStruct((n, sectors, rows, width), bf16),
        in_specs=[smem_spec] * 3 + [vmem_spec] * 4,
        out_specs=vmem_spec,
        compiler_params=params,
        cost_estimate=pl.CostEstimate(flops=2 * sectors * width**3, bytes_accessed=2 * 2 * sectors * width**2, transcendentals=0),
    )(scal, shifts, sector_sizes, left_rows, wavefunction, near, far)

    psi_1, low_1 = pl.pallas_call(
        functools.partial(iter1_kernel, slots),
        out_shape=(
            jax.ShapeDtypeStruct((sectors, rows, cols), f32),
            jax.ShapeDtypeStruct((sectors, rows, cols), bf16),
        ),
        in_specs=[smem_spec] * 4 + [vmem_spec] + [any_spec] * (3 + n_slots),
        out_specs=(vmem_spec, vmem_spec),
        scratch_shapes=[
            pltpu.VMEM((n, cols, width), bf16),
            pltpu.VMEM((sectors, rows, cols), bf16),
            pltpu.VMEM((sectors * rows, cols), f32),
            pltpu.SemaphoreType.DMA((n_slots + 3,)),
        ],
        compiler_params=params,
        cost_estimate=pl.CostEstimate(flops=2 * sectors * width**2 * cols, bytes_accessed=2 * 2 * sectors * width**2, transcendentals=0),
    )(scal, table, sector_sizes, factors[:1], inner, wavefunction, near, far, *right_pieces)

    chunk = jnp.stack([low_1, swap_sec(low_1)])
    psi_pieces = ring_gather(chunk, n)

    below = lax.ppermute(left_ops[0], "ops", [(i, i + 1) for i in range(n - 1)])
    above = lax.ppermute(left_ops[0], "ops", [(i + 1, i) for i in range(n - 1)])
    mixer = (
        integrals[0, 0] * below.astype(f32)
        + integrals[0, 1] * left_ops[0].astype(f32)
        + integrals[0, 2] * above.astype(f32)
    ).astype(bf16)

    message = (local + 1) * rows + 16
    keep, send = pl.pallas_call(
        functools.partial(iter2_kernel, slots),
        out_shape=(jax.ShapeDtypeStruct((message, cols), bf16),) * 2,
        in_specs=[smem_spec] * 5 + [vmem_spec] * 2 + [any_spec] * (2 * n_slots),
        out_specs=(vmem_spec, vmem_spec),
        scratch_shapes=[
            pltpu.VMEM((2, sectors, width, cols), bf16),
            pltpu.VMEM((n, sectors, rows, width), bf16),
            pltpu.VMEM((n, cols, width), bf16),
            pltpu.VMEM((sectors * rows, cols), f32),
            pltpu.VMEM((sectors, rows, cols), bf16),
            pltpu.SemaphoreType.DMA((2 * n,)),
            pltpu.SemaphoreType.DMA((n_slots,)),
        ],
        compiler_params=params,
        cost_estimate=pl.CostEstimate(flops=3 * sectors * width**3, bytes_accessed=2 * 2 * sectors * width**2, transcendentals=0),
    )(scal, table, shifts, sector_sizes, factors[1:2], left_rows, psi_1, *psi_pieces, *right_pieces)

    last = jnp.stack([keep, swap_sec(send)])
    last_pieces = ring_gather(last, n)

    wave, mixed = pl.pallas_call(
        functools.partial(final_kernel, slots, float(sectors * width * width)),
        out_shape=(
            jax.ShapeDtypeStruct((local, width, width), f32),
            jax.ShapeDtypeStruct((width, cols), bf16),
        ),
        in_specs=[smem_spec] * 2 + [vmem_spec] * (1 + n_slots),
        out_specs=(vmem_spec, vmem_spec),
        scratch_shapes=[pltpu.VMEM((width, width), bf16), pltpu.SemaphoreType.DMA((1,))],
        compiler_params=params,
        cost_estimate=pl.CostEstimate(flops=2 * width**3, bytes_accessed=6 * local * width**2, transcendentals=0),
    )(scal, table, mixer, *last_pieces)
    return (wave, mixed[None])


def shards(wavefunction, left_ops, right_ops, *rest):
    n, halves = lax.axis_size("ops"), lax.axis_size("sec")
    width = right_ops.shape[1]
    gathered = 2 * n * right_ops.size // halves
    fits = gathered <= GATHER_BYTES and halves == 2 and right_ops.shape[0] == 1
    aligned = n % 4 == 0 and width % (16 * n) == 0 and width % 256 == 0 and wavefunction.shape[0] % 2 == 0
    form = gather_form if fits and aligned else reduce_form
    return form(wavefunction, left_ops, right_ops, *rest)


def solution(mesh):
    placed = (
        P("sec", None, None),
        P("ops", None, None),
        P("ops", None, None),
        P("ops"),
        P(),
        P(),
        P("ops", None),
    )
    return jax.shard_map(
        shards,
        mesh=mesh,
        in_specs=placed,
        out_specs=(P("sec", None, None), P("ops", None, "sec")),
        check_vma=False,
    )
```

```python
import functools
import math

import jax
import jax.numpy as jnp
import numpy as np
from jax import lax
from jax.experimental import pallas as pl
from jax.experimental.pallas import tpu as pltpu
from jax.sharding import PartitionSpec as P


ITERS = 2
GATHER_BYTES = 8 * 1024 * 1024
VMEM = pltpu.MemorySpace.VMEM
SMEM = pltpu.MemorySpace.SMEM


def broadcast(value, axis, source):
    kept = jnp.where(lax.axis_index(axis) == source, value, 0).astype(value.dtype)
    return lax.psum(kept, axis)


def padded_2(cells, sides, width):
    for axis, dim in sides:
        count = lax.axis_size(axis)
        ends = count - 1
        head = lax.slice_in_dim(cells, 0, width, axis=dim)
        tail = lax.slice_in_dim(cells, cells.shape[dim] - width, cells.shape[dim], axis=dim)
        cells = jnp.concatenate(
            [
                lax.ppermute(tail, axis, [(i, (i + 1) % count) for i in range(ends)]),
                cells,
                lax.ppermute(head, axis, [((i + 1) % count, i) for i in range(ends)]),
            ],
            axis=dim,
        )
    return cells


def reduce_form(wavefunction, left_ops, right_ops, shift_map, sector_sizes, step_sizes, integrals):
    highest = lax.Precision.HIGHEST
    local_sec = wavefunction.shape[0]
    width = wavefunction.shape[1]
    sectors = sector_sizes.shape[0]
    count = lax.axis_size("ops") * left_ops.shape[0]
    first = lax.axis_index("sec") * local_sec
    local_sizes = lax.dynamic_slice_in_dim(sector_sizes, first, local_sec, 0)
    column = jnp.arange(width, dtype=jnp.int32)
    row_ok = (column[None, :] < local_sizes[:, None]).astype(jnp.float32)
    mask = row_ok[:, :, None] * row_ok[:, None, :]
    psi = wavefunction.astype(jnp.float32) * mask
    sources = first + jnp.arange(local_sec, dtype=jnp.int32)
    target = (sources[None, :] + shift_map[:, None]) % sectors
    routing = (jnp.arange(sectors, dtype=jnp.int32)[:, None, None] == target[None]).astype(
        jnp.float32
    )
    for step in range(ITERS):
        psi_low = psi.astype(jnp.bfloat16)
        inner = jnp.einsum(
            "kmn,snp->ksmp", left_ops, psi_low, preferred_element_type=jnp.float32
        ).astype(jnp.bfloat16)
        terms = jnp.einsum("ksmp,kqp->ksmq", inner, right_ops, preferred_element_type=jnp.float32)
        contrib = jnp.einsum("tks,ksmq->tmq", routing, terms, precision=highest)
        partial_rows = lax.psum_scatter(contrib, "ops", scatter_dimension=1, tiled=True)
        own_rows = lax.psum_scatter(
            partial_rows.astype(jnp.bfloat16), "sec", scatter_dimension=0, tiled=True
        ).astype(jnp.float32)
        hpsi = lax.all_gather(own_rows.astype(jnp.bfloat16), "ops", axis=1, tiled=True).astype(
            own_rows.dtype
        )
        factor = step_sizes[step].astype(jnp.float32) / (8.0 * math.sqrt(count))
        psi = mask * (psi - factor * hpsi)
        total = lax.psum(jnp.sum(psi * psi), "sec")
        psi = psi / jnp.sqrt(total / (sectors * width * width) + 1e-06)
    basis = broadcast(psi[0].astype(jnp.bfloat16), "sec", 0)
    col_count = width // lax.axis_size("sec")
    basis_cols = lax.dynamic_slice_in_dim(basis, lax.axis_index("sec") * col_count, col_count, 1)
    half = jnp.einsum("mp,kmn->kpn", basis, left_ops, preferred_element_type=jnp.float32).astype(
        jnp.bfloat16
    )
    rotated = (
        jnp.einsum("kpn,nq->kpq", half, basis_cols, preferred_element_type=jnp.float32) / width
    )
    padded = padded_2(rotated.astype(jnp.bfloat16), (("ops", 0),), 1).astype(rotated.dtype)
    mixed = (
        integrals[:, 0, None, None] * padded[:-2]
        + integrals[:, 1, None, None] * padded[1:-1]
        + integrals[:, 2, None, None] * padded[2:]
    )
    return (psi, mixed.astype(jnp.bfloat16))


def ring_order(chips):
    return list(range(0, chips, 2)) + list(range(chips - 1, 0, -2))


def swap_core(x, n):
    return lax.ppermute(x, "ops", [(o, o ^ 1) for o in range(n)])


def swap_sec(x):
    return lax.ppermute(x, "sec", [(0, 1), (1, 0)])


def along_ring(x, n, by):
    order = ring_order(n // 2)
    place = {chip: i for i, chip in enumerate(order)}
    perm = []
    for o in range(n):
        chip = order[(place[o // 2] + by) % len(order)]
        perm.append((o, 2 * chip + o % 2))
    return lax.ppermute(x, "ops", perm)


def ring_slots(n):
    slots = [(0, 0)]
    for step in range(1, n // 4):
        slots += [(-step, 0), (step, 0)]
    slots.append((-(n // 4), 0))
    return slots + [(d, 1) for d, _ in slots]


def ring_table(n):
    order = ring_order(n // 2)
    place = {chip: i for i, chip in enumerate(order)}
    rows = []
    for o in range(n):
        at = place[o // 2]
        rows.append([2 * order[(at + d) % len(order)] + ((o % 2) ^ c) for d, c in ring_slots(n)])
    return np.array(rows, np.int32)


def ring_gather(x, n):
    last = n // 4
    up = down = x
    own = [x]
    for step in range(1, last + 1):
        up = along_ring(up, n, 1)
        own.append(up)
        if step < last:
            down = along_ring(down, n, -1)
            own.append(down)
    other = []
    for piece in own:
        other.append(swap_core(piece, n))
    return own + other


def copy_in(pairs, sems):
    copies = []
    for i, (src, dst) in enumerate(pairs):
        copy = pltpu.make_async_copy(src, dst, sems.at[i])
        copy.start()
        copies.append(copy)
    return copies


def wait_all(copies):
    for copy in copies:
        copy.wait()


def cut_psi(psi, size):
    row = lax.broadcasted_iota(jnp.int32, (psi.shape[0], 1), 0)
    col = lax.broadcasted_iota(jnp.int32, (1, psi.shape[1]), 1)
    rows = jnp.where(row < size, 1.0, 0.0).astype(psi.dtype)
    cols = jnp.where(col < size, 1.0, 0.0).astype(psi.dtype)
    return psi * rows * cols


def first_stage(left_ref, psi, inner_shape):
    product = jnp.dot(left_ref[...], psi, preferred_element_type=jnp.float32).astype(jnp.bfloat16)
    return product.reshape(inner_shape[0], inner_shape[2], psi.shape[1])


def own_kernel(scal_ref, sizes_ref, left_ref, wave_ref, out_ref, waves, sems):
    local = wave_ref.shape[0]
    copies = copy_in([(wave_ref.at[i], waves.at[i]) for i in range(local)], sems)
    for i in range(local):
        copies[i].wait()
        psi = cut_psi(waves[i], sizes_ref[scal_ref[2] * local + i])
        out_ref[:, i] = first_stage(left_ref, psi, out_ref.shape)


def second_stage(terms, right, cols):
    total = None
    for i, inner in enumerate(terms):
        sectors, _, _ = inner.shape
        shift = jnp.max(right[i, cols:, :128].astype(jnp.float32)).astype(jnp.int32)
        rhs = right[i, :cols]
        lhs = jnp.concatenate([inner[lax.rem(t - shift + sectors, sectors)] for t in range(sectors)], axis=0)
        product = lax.dot_general(
            lhs, rhs, (((1,), (1,)), ((), ())), preferred_element_type=jnp.float32
        )
        total = product if total is None else total + product
    return total


def step_rows(psi, acc, sizes_ref, scal_ref, factor, sector):
    rows, cols = psi.shape
    size = sizes_ref[sector]
    row = lax.broadcasted_iota(jnp.int32, psi.shape, 0) + scal_ref[0] * rows
    col = lax.broadcasted_iota(jnp.int32, psi.shape, 1) + scal_ref[2] * cols
    moved = psi - factor * acc[sector * rows : (sector + 1) * rows]
    return jnp.where((row < size) & (col < size), moved, 0.0)


def early_kernel(early, late, *refs):
    scal_ref, table_ref, sizes_ref, left_ref, own_ref, near_ref, far_ref = refs[:7]
    pieces = refs[7 : 7 + len(early)]
    acc_ref, rest_ref, right, inner, waves, wsems, rsems, isem = refs[7 + len(early) :]
    core, sec = scal_ref[1], scal_ref[2]
    cols = acc_ref.shape[1]
    local = own_ref.shape[1]
    half = local // 2
    sources = [(near_ref.at[i], waves.at[i]) for i in range(half)]
    sources += [(far_ref.at[i], waves.at[half + i]) for i in range(half)]
    wave_copies = copy_in(sources, wsems)
    copies = copy_in([(own_ref, inner.at[:, pl.ds(sec * local, local)])], isem)
    copies += copy_in([(piece, right.at[i]) for i, piece in enumerate(pieces)], rsems)
    foreign = (1 - sec) * local
    swapped = core * half

    for slot in range(local):
        wave_copies[slot].wait()
        sector = foreign + lax.rem(swapped + slot, local)
        psi = cut_psi(waves[slot], sizes_ref[sector])
        inner[:, sector] = first_stage(left_ref, psi, inner.shape)

    wait_all(copies)
    acc_ref[...] = second_stage([inner.at[table_ref[i]] for i in early], right, cols)
    for at, i in enumerate(late):
        rest_ref[at] = inner[table_ref[i]]


def late_kernel(*refs):
    scal_ref, sizes_ref, factor_ref, acc_ref, rest_ref, own_ref, near_ref, far_ref = refs[:8]
    pieces = refs[8:10]
    out_ref, send_ref, right, start, rsems, ssems = refs[10:]
    o, core, sec = scal_ref[0], scal_ref[1], scal_ref[2]
    local = own_ref.shape[0]
    _, rows, cols = out_ref.shape
    here = (slice(None), pl.ds(o * rows, rows), pl.ds(sec * cols, cols))
    foreign, half = (1 - sec) * local, local // 2
    copies = copy_in([(piece, right.at[c]) for c, piece in enumerate(pieces)], rsems)
    copies += copy_in(
        [
            (own_ref.at[here], start.at[pl.ds(sec * local, local)]),
            (near_ref.at[here], start.at[pl.ds(foreign + core * half, half)]),
            (far_ref.at[here], start.at[pl.ds(foreign + (1 - core) * half, half)]),
        ],
        ssems,
    )
    wait_all(copies)
    acc = acc_ref[...] + second_stage([rest_ref.at[c] for c in range(2)], right, cols)
    for s in range(out_ref.shape[0]):
        moved = step_rows(start[s].astype(jnp.float32), acc, sizes_ref, scal_ref, factor_ref[0], s)
        out_ref[s] = moved
        send_ref[s] = moved.astype(jnp.bfloat16)


def split_3(value):
    parts = []
    for _ in range(3):
        low = value.astype(jnp.bfloat16)
        parts.append(low)
        value = value - low.astype(jnp.float32)
    return parts


def iter2_kernel(slots, *refs):
    n_slots = len(slots)
    scal_ref, table_ref, sizes_ref, factor_ref, left_ref, prev_ref = refs[:6]
    psi_pieces = refs[6 : 6 + n_slots]
    right_pieces = refs[6 + n_slots : 6 + 2 * n_slots]
    keep_ref, send_ref, psi, inner, right, low, psems, rsems = refs[6 + 2 * n_slots :]
    sec = scal_ref[2]
    sectors, rows, cols = prev_ref.shape
    local = sectors // 2
    pairs = []
    for i, piece in enumerate(psi_pieces):
        at = pl.ds(table_ref[i] * rows, rows)
        pairs += [(piece.at[h], psi.at[sec if h == 0 else 1 - sec, :, at]) for h in range(2)]
    psi_copies = copy_in(pairs, psems)
    right_copies = copy_in([(piece, right.at[i]) for i, piece in enumerate(right_pieces)], rsems)
    wait_all(psi_copies)

    @pl.loop(0, sectors, unroll=2)
    def _(s):
        for h in range(2):
            inner[:, s, :, h * cols : (h + 1) * cols] = first_stage(left_ref, psi[h, s], inner.shape)

    wait_all(right_copies)
    acc = second_stage([inner.at[table_ref[i]] for i in range(n_slots)], right, cols)
    before = jnp.zeros((rows, cols), jnp.float32)
    after = jnp.zeros((rows, cols), jnp.float32)
    for s in range(sectors):
        old = prev_ref[s]
        moved = step_rows(old, acc, sizes_ref, scal_ref, factor_ref[0], s)
        low[s] = moved.astype(jnp.bfloat16)
        before += old * old
        after += moved * moved
    for i in range(local):
        keep_ref[i * rows : (i + 1) * rows] = low[sec * local + i]
        send_ref[i * rows : (i + 1) * rows] = low[(1 - sec) * local + i]
    keep_ref[local * rows : (local + 1) * rows] = low[0]
    send_ref[local * rows : (local + 1) * rows] = low[0]
    tail = keep_ref.shape[0] - (local + 1) * rows
    line = lax.broadcasted_iota(jnp.int32, (tail, cols), 0)
    stats = jnp.zeros((tail, cols), jnp.float32)
    for i, total in enumerate((before, after)):
        parts = split_3(jnp.full((tail, cols), jnp.sum(total), jnp.float32))
        for p, low_part in enumerate(parts):
            stats = jnp.where(line == 3 * i + p, low_part.astype(jnp.float32), stats)
    keep_ref[(local + 1) * rows :] = stats.astype(jnp.bfloat16)
    send_ref[(local + 1) * rows :] = stats.astype(jnp.bfloat16)


def final_kernel(slots, values, *refs):
    n_slots = len(slots)
    scal_ref, table_ref, mixer_ref = refs[:3]
    pieces = refs[3 : 3 + n_slots]
    wave_ref, mixed_ref, basis = refs[3 + n_slots :]
    sec = scal_ref[2]
    local, width, _ = wave_ref.shape
    cols = width // 2
    rows = width // n_slots
    tail = pieces[0].shape[1] - (local + 1) * rows
    stats = jnp.zeros((tail, cols), jnp.float32)
    views = []
    for i, piece in enumerate(pieces):
        at = pl.ds(pl.multiple_of(table_ref[i] * rows, rows), rows)
        for h in range(2):
            side = sec if h == 0 else 1 - sec
            across = pl.ds(pl.multiple_of(side * cols, cols), cols)
            view = piece.at[h]
            views.append((view, at, across))
            stats += view[(local + 1) * rows :].astype(jnp.float32)
            basis[at, across] = view[local * rows : (local + 1) * rows]
    line = lax.broadcasted_iota(jnp.int32, (tail, cols), 0)
    first = jnp.sum(jnp.where(line < 3, stats, 0.0), axis=0, keepdims=True)[:, :1]
    second = jnp.sum(jnp.where((line >= 3) & (line < 6), stats, 0.0), axis=0, keepdims=True)[:, :1]
    norm_1 = jnp.sqrt(first / values + 1e-06)
    norm_2 = jnp.sqrt(second / (norm_1 * norm_1) / values + 1e-06)
    scale = 1.0 / (norm_1 * norm_2)
    for s in range(local):
        for view, at, across in views:
            wave_ref[s, at, across] = view[s * rows : (s + 1) * rows].astype(jnp.float32) * scale
    across = pl.ds(pl.multiple_of(sec * cols, cols), cols)
    right = jnp.dot(mixer_ref[...], basis[:, across], preferred_element_type=jnp.float32)
    rotated = lax.dot_general(
        basis[...], right.astype(jnp.bfloat16), (((0,), (0,)), ((), ())), preferred_element_type=jnp.float32
    )
    mixed_ref[...] = (rotated * (scale * scale / width)).astype(jnp.bfloat16)


def kernel_call(body, out, ins, scratch, mib, flops, moved):
    spaces = {"s": SMEM, "v": VMEM, "a": pl.ANY, "h": pltpu.MemorySpace.HBM}
    multiple = isinstance(out, (tuple, list))
    out_spec = pl.BlockSpec(memory_space=VMEM)
    return pl.pallas_call(
        body,
        out_shape=out,
        in_specs=[pl.BlockSpec(memory_space=spaces[c]) for c in ins],
        out_specs=(out_spec,) * len(out) if multiple else out_spec,
        scratch_shapes=scratch,
        compiler_params=pltpu.CompilerParams(vmem_limit_bytes=mib * 1024 * 1024),
        cost_estimate=pl.CostEstimate(flops=flops, bytes_accessed=moved, transcendentals=0),
    )


def gather_form(wavefunction, left_ops, right_ops, shift_map, sector_sizes, step_sizes, integrals):
    f32, bf16 = jnp.float32, jnp.bfloat16
    n = lax.axis_size("ops")
    local, width, _ = wavefunction.shape
    sectors = sector_sizes.shape[0]
    rows, cols = width // n, width // 2
    o, sec = lax.axis_index("ops"), lax.axis_index("sec")
    core = lax.rem(o, 2)
    slots = ring_slots(n)
    n_slots = len(slots)
    late = [n_slots // 2 - 1, n_slots - 1]
    early = [i for i in range(n_slots) if i not in late]
    scal = jnp.stack([o, core, sec]).astype(jnp.int32)
    table = lax.dynamic_slice_in_dim(jnp.asarray(ring_table(n)), o, 1, 0)[0]
    factors = step_sizes.astype(f32) / (8.0 * math.sqrt(n))
    shape = jax.ShapeDtypeStruct
    dma = pltpu.SemaphoreType.DMA
    psi_bytes = 2 * sectors * width**2
    tall = cols + 16

    right_cols = jnp.concatenate(
        [
            lax.dynamic_slice_in_dim(right_ops[0], sec * cols, cols, 0),
            jnp.broadcast_to(shift_map.astype(bf16)[:, None], (16, width)),
        ]
    )
    right_pieces = ring_gather(right_cols, n)
    left_rows = lax.all_to_all(left_ops[0], "ops", 0, 0, tiled=True)
    part = lax.dynamic_slice_in_dim(wavefunction, core * (local // 2), local // 2, 0)
    near = swap_sec(part)
    far = swap_core(near, n)

    inner = kernel_call(
        own_kernel, shape((n, local, rows, width), bf16), "ssva",
        [pltpu.VMEM((local, width, width), bf16), dma((local,))],
        10, sectors * width**3, psi_bytes,
    )(scal, sector_sizes, left_rows, wavefunction)
    acc, rest = kernel_call(
        functools.partial(early_kernel, early, late),
        (shape((sectors * rows, cols), f32), shape((2, sectors, rows, width), bf16)),
        "sssvaaa" + "a" * len(early),
        [
            pltpu.VMEM((len(early), tall, width), bf16),
            pltpu.VMEM((n, sectors, rows, width), bf16),
            pltpu.VMEM((local, width, width), bf16),
            dma((local,)),
            dma((len(early),)),
            dma((1,)),
        ],
        16, 2 * sectors * width**2 * cols, 2 * psi_bytes,
    )(scal, table, sector_sizes, left_rows, inner, near, far, *[right_pieces[i] for i in early])
    psi_1, low_1 = kernel_call(
        late_kernel,
        (shape((sectors, rows, cols), f32), shape((sectors, rows, cols), bf16)),
        "sssvvaaaaa",
        [pltpu.VMEM((2, tall, width), bf16), pltpu.VMEM((sectors, rows, cols), bf16), dma((2,)), dma((3,))],
        8, sectors * width * cols * cols, psi_bytes // 4,
    )(scal, sector_sizes, factors[:1], acc, rest, wavefunction, near, far, *[right_pieces[i] for i in late])

    low_2 = swap_sec(low_1)
    below = lax.ppermute(left_ops[0], "ops", [(i, i + 1) for i in range(n - 1)])
    above = lax.ppermute(left_ops[0], "ops", [(i + 1, i) for i in range(n - 1)])
    psi_pieces = ring_gather(jnp.stack([low_1, low_2]), n)
    mixer = (
        integrals[0, 0] * below.astype(f32)
        + integrals[0, 1] * left_ops[0].astype(f32)
        + integrals[0, 2] * above.astype(f32)
    ).astype(bf16)

    message = (local + 1) * rows + 16
    keep, send = kernel_call(
        functools.partial(iter2_kernel, slots), (shape((message, cols), bf16),) * 2,
        "ssssvv" + "a" * (2 * n_slots),
        [
            pltpu.VMEM((2, sectors, width, cols), bf16),
            pltpu.VMEM((n, sectors, rows, width), bf16),
            pltpu.VMEM((n, tall, width), bf16),
            pltpu.VMEM((sectors, rows, cols), bf16),
            dma((2 * n_slots,)),
            dma((n_slots,)),
        ],
        18, 3 * sectors * width**3, 2 * psi_bytes,
    )(scal, table, sector_sizes, factors[1:2], left_rows, psi_1, *psi_pieces, *right_pieces)

    recv = swap_sec(send)
    last_pieces = ring_gather(jnp.stack([keep, recv]), n)
    wave, mixed = kernel_call(
        functools.partial(final_kernel, slots, float(sectors * width * width)),
        (shape((local, width, width), f32), shape((width, cols), bf16)),
        "ssv" + "v" * n_slots, [pltpu.VMEM((width, width), bf16)],
        16, 2 * width**3, 6 * local * width**2,
    )(scal, table, mixer, *last_pieces)
    return (wave, mixed[None])


def shards(wavefunction, left_ops, right_ops, *rest):
    n, halves = lax.axis_size("ops"), lax.axis_size("sec")
    width = right_ops.shape[1]
    gathered = 2 * n * right_ops.size // halves
    fits = gathered <= GATHER_BYTES and halves == 2 and right_ops.shape[0] == 1
    aligned = n % 4 == 0 and width % (16 * n) == 0 and width % 256 == 0 and wavefunction.shape[0] % 2 == 0
    form = gather_form if fits and aligned else reduce_form
    return form(wavefunction, left_ops, right_ops, *rest)


def solution(mesh):
    placed = (
        P("sec", None, None),
        P("ops", None, None),
        P("ops", None, None),
        P("ops"),
        P(),
        P(),
        P("ops", None),
    )
    return jax.shard_map(
        shards,
        mesh=mesh,
        in_specs=placed,
        out_specs=(P("sec", None, None), P("ops", None, "sec")),
        check_vma=False,
    )
```

```python
import functools
import math

import jax
import jax.numpy as jnp
import numpy as np
from jax import lax
from jax.experimental import pallas as pl
from jax.experimental.pallas import tpu as pltpu
from jax.sharding import PartitionSpec as P


ITERS = 2
GATHER_BYTES = 8 * 1024 * 1024
VMEM = pltpu.MemorySpace.VMEM
SMEM = pltpu.MemorySpace.SMEM


def broadcast(value, axis, source):
    kept = jnp.where(lax.axis_index(axis) == source, value, 0).astype(value.dtype)
    return lax.psum(kept, axis)


def padded_2(cells, sides, width):
    for axis, dim in sides:
        count = lax.axis_size(axis)
        ends = count - 1
        head = lax.slice_in_dim(cells, 0, width, axis=dim)
        tail = lax.slice_in_dim(cells, cells.shape[dim] - width, cells.shape[dim], axis=dim)
        cells = jnp.concatenate(
            [
                lax.ppermute(tail, axis, [(i, (i + 1) % count) for i in range(ends)]),
                cells,
                lax.ppermute(head, axis, [((i + 1) % count, i) for i in range(ends)]),
            ],
            axis=dim,
        )
    return cells


def reduce_form(wavefunction, left_ops, right_ops, shift_map, sector_sizes, step_sizes, integrals):
    highest = lax.Precision.HIGHEST
    local_sec = wavefunction.shape[0]
    width = wavefunction.shape[1]
    sectors = sector_sizes.shape[0]
    count = lax.axis_size("ops") * left_ops.shape[0]
    first = lax.axis_index("sec") * local_sec
    local_sizes = lax.dynamic_slice_in_dim(sector_sizes, first, local_sec, 0)
    column = jnp.arange(width, dtype=jnp.int32)
    row_ok = (column[None, :] < local_sizes[:, None]).astype(jnp.float32)
    mask = row_ok[:, :, None] * row_ok[:, None, :]
    psi = wavefunction.astype(jnp.float32) * mask
    sources = first + jnp.arange(local_sec, dtype=jnp.int32)
    target = (sources[None, :] + shift_map[:, None]) % sectors
    routing = (jnp.arange(sectors, dtype=jnp.int32)[:, None, None] == target[None]).astype(
        jnp.float32
    )
    for step in range(ITERS):
        psi_low = psi.astype(jnp.bfloat16)
        inner = jnp.einsum(
            "kmn,snp->ksmp", left_ops, psi_low, preferred_element_type=jnp.float32
        ).astype(jnp.bfloat16)
        terms = jnp.einsum("ksmp,kqp->ksmq", inner, right_ops, preferred_element_type=jnp.float32)
        contrib = jnp.einsum("tks,ksmq->tmq", routing, terms, precision=highest)
        partial_rows = lax.psum_scatter(contrib, "ops", scatter_dimension=1, tiled=True)
        own_rows = lax.psum_scatter(
            partial_rows.astype(jnp.bfloat16), "sec", scatter_dimension=0, tiled=True
        ).astype(jnp.float32)
        hpsi = lax.all_gather(own_rows.astype(jnp.bfloat16), "ops", axis=1, tiled=True).astype(
            own_rows.dtype
        )
        factor = step_sizes[step].astype(jnp.float32) / (8.0 * math.sqrt(count))
        psi = mask * (psi - factor * hpsi)
        total = lax.psum(jnp.sum(psi * psi), "sec")
        psi = psi / jnp.sqrt(total / (sectors * width * width) + 1e-06)
    basis = broadcast(psi[0].astype(jnp.bfloat16), "sec", 0)
    col_count = width // lax.axis_size("sec")
    basis_cols = lax.dynamic_slice_in_dim(basis, lax.axis_index("sec") * col_count, col_count, 1)
    half = jnp.einsum("mp,kmn->kpn", basis, left_ops, preferred_element_type=jnp.float32).astype(
        jnp.bfloat16
    )
    rotated = (
        jnp.einsum("kpn,nq->kpq", half, basis_cols, preferred_element_type=jnp.float32) / width
    )
    padded = padded_2(rotated.astype(jnp.bfloat16), (("ops", 0),), 1).astype(rotated.dtype)
    mixed = (
        integrals[:, 0, None, None] * padded[:-2]
        + integrals[:, 1, None, None] * padded[1:-1]
        + integrals[:, 2, None, None] * padded[2:]
    )
    return (psi, mixed.astype(jnp.bfloat16))


def ring_order(chips):
    return list(range(0, chips, 2)) + list(range(chips - 1, 0, -2))


def swap_core(x, n):
    return lax.ppermute(x, "ops", [(o, o ^ 1) for o in range(n)])


def swap_sec(x):
    return lax.ppermute(x, "sec", [(0, 1), (1, 0)])


def along_ring(x, n, by):
    order = ring_order(n // 2)
    place = {chip: i for i, chip in enumerate(order)}
    perm = []
    for o in range(n):
        chip = order[(place[o // 2] + by) % len(order)]
        perm.append((o, 2 * chip + o % 2))
    return lax.ppermute(x, "ops", perm)


def ring_slots(n):
    slots = [(0, 0)]
    for step in range(1, n // 4):
        slots += [(-step, 0), (step, 0)]
    slots.append((-(n // 4), 0))
    return slots + [(d, 1) for d, _ in slots]


def ring_table(n):
    order = ring_order(n // 2)
    place = {chip: i for i, chip in enumerate(order)}
    rows = []
    for o in range(n):
        at = place[o // 2]
        rows.append([2 * order[(at + d) % len(order)] + ((o % 2) ^ c) for d, c in ring_slots(n)])
    return np.array(rows, np.int32)


def ring_gather(x, n):
    last = n // 4
    up = down = x
    own = [x]
    for step in range(1, last + 1):
        up = along_ring(up, n, 1)
        own.append(up)
        if step < last:
            down = along_ring(down, n, -1)
            own.append(down)
    other = []
    for piece in own:
        other.append(swap_core(piece, n))
    return own + other


def copy_in(pairs, sems):
    copies = []
    for i, (src, dst) in enumerate(pairs):
        copy = pltpu.make_async_copy(src, dst, sems.at[i])
        copy.start()
        copies.append(copy)
    return copies


def wait_all(copies):
    for copy in copies:
        copy.wait()


def cut_psi(psi, size):
    row = lax.broadcasted_iota(jnp.int32, (psi.shape[0], 1), 0)
    col = lax.broadcasted_iota(jnp.int32, (1, psi.shape[1]), 1)
    rows = jnp.where(row < size, 1.0, 0.0).astype(psi.dtype)
    cols = jnp.where(col < size, 1.0, 0.0).astype(psi.dtype)
    return psi * rows * cols


def first_stage(left_ref, psi, inner_shape):
    product = jnp.dot(left_ref[...], psi, preferred_element_type=jnp.float32).astype(jnp.bfloat16)
    return product.reshape(inner_shape[0], inner_shape[2], psi.shape[1])


def own_kernel(scal_ref, sizes_ref, left_ref, wave_ref, out_ref, waves, sems):
    local = wave_ref.shape[0]
    copies = copy_in([(wave_ref.at[i], waves.at[i]) for i in range(local)], sems)
    for i in range(local):
        copies[i].wait()
        psi = cut_psi(waves[i], sizes_ref[scal_ref[2] * local + i])
        out_ref[:, i] = first_stage(left_ref, psi, out_ref.shape)


def second_stage(terms, right, cols):
    total = None
    for i, inner in enumerate(terms):
        sectors, _, _ = inner.shape
        shift = jnp.max(right[i, cols:, :128].astype(jnp.float32)).astype(jnp.int32)
        rhs = right[i, :cols]
        lhs = jnp.concatenate([inner[lax.rem(t - shift + sectors, sectors)] for t in range(sectors)], axis=0)
        product = lax.dot_general(
            lhs, rhs, (((1,), (1,)), ((), ())), preferred_element_type=jnp.float32
        )
        total = product if total is None else total + product
    return total


def step_rows(psi, acc, sizes_ref, scal_ref, factor, sector):
    rows, cols = psi.shape
    size = sizes_ref[sector]
    row = lax.broadcasted_iota(jnp.int32, psi.shape, 0) + scal_ref[0] * rows
    col = lax.broadcasted_iota(jnp.int32, psi.shape, 1) + scal_ref[2] * cols
    moved = psi - factor * acc[sector * rows : (sector + 1) * rows]
    return jnp.where((row < size) & (col < size), moved, 0.0)


def early_kernel(early, late, *refs):
    scal_ref, table_ref, sizes_ref, left_ref, own_ref, near_ref, far_ref = refs[:7]
    pieces = refs[7 : 7 + len(early)]
    acc_ref, rest_ref, right, inner, waves, wsems, rsems, isem = refs[7 + len(early) :]
    core, sec = scal_ref[1], scal_ref[2]
    cols = acc_ref.shape[1]
    local = own_ref.shape[1]
    half = local // 2
    sources = [(near_ref.at[i], waves.at[i]) for i in range(half)]
    sources += [(far_ref.at[i], waves.at[half + i]) for i in range(half)]
    wave_copies = copy_in(sources, wsems)
    copies = copy_in([(own_ref, inner.at[:, pl.ds(sec * local, local)])], isem)
    copies += copy_in([(piece, right.at[i]) for i, piece in enumerate(pieces)], rsems)
    foreign = (1 - sec) * local
    swapped = core * half

    for slot in range(local):
        wave_copies[slot].wait()
        sector = foreign + lax.rem(swapped + slot, local)
        psi = cut_psi(waves[slot], sizes_ref[sector])
        inner[:, sector] = first_stage(left_ref, psi, inner.shape)

    wait_all(copies)
    acc_ref[...] = second_stage([inner.at[table_ref[i]] for i in early], right, cols)
    for at, i in enumerate(late):
        rest_ref[at] = inner[table_ref[i]]


def late_kernel(*refs):
    scal_ref, sizes_ref, factor_ref, acc_ref, rest_ref, own_ref, near_ref, far_ref = refs[:8]
    pieces = refs[8:10]
    out_ref, send_ref, right, start, rsems, ssems = refs[10:]
    o, core, sec = scal_ref[0], scal_ref[1], scal_ref[2]
    local = own_ref.shape[0]
    _, rows, cols = out_ref.shape
    here = (slice(None), pl.ds(o * rows, rows), pl.ds(sec * cols, cols))
    foreign, half = (1 - sec) * local, local // 2
    copies = copy_in([(piece, right.at[c]) for c, piece in enumerate(pieces)], rsems)
    copies += copy_in(
        [
            (own_ref.at[here], start.at[pl.ds(sec * local, local)]),
            (near_ref.at[here], start.at[pl.ds(foreign + core * half, half)]),
            (far_ref.at[here], start.at[pl.ds(foreign + (1 - core) * half, half)]),
        ],
        ssems,
    )
    wait_all(copies)
    acc = acc_ref[...] + second_stage([rest_ref.at[c] for c in range(2)], right, cols)
    for s in range(out_ref.shape[0]):
        moved = step_rows(start[s].astype(jnp.float32), acc, sizes_ref, scal_ref, factor_ref[0], s)
        out_ref[s] = moved
        send_ref[s] = moved.astype(jnp.bfloat16)


def split_3(value):
    parts = []
    for _ in range(3):
        low = value.astype(jnp.bfloat16)
        parts.append(low)
        value = value - low.astype(jnp.float32)
    return parts


def iter2_kernel(n_slots, early, late, *refs):
    scal_ref, table_ref, sizes_ref, factor_ref, left_ref, prev_ref = refs[:6]
    psi_pieces = refs[6 : 6 + 2 * n_slots]
    right_pieces = refs[6 + 2 * n_slots : 9 + 2 * n_slots]
    keep_ref, send_ref, psi, inner, right, low, psems, rsems = refs[9 + 2 * n_slots :]
    sec = scal_ref[2]
    sectors, rows, cols = prev_ref.shape
    local = sectors // 2
    pairs = []
    for i, piece in enumerate(psi_pieces):
        at = pl.ds(table_ref[i % n_slots] * rows, rows)
        pairs.append((piece, psi.at[sec if i < n_slots else 1 - sec, :, at]))
    psi_copies = copy_in(pairs, psems)
    right_copies = copy_in(
        [(right_pieces[0], right.at[pl.ds(0, len(early))])]
        + [(right_pieces[1 + c], right.at[len(early) + c]) for c in range(2)],
        rsems,
    )
    wait_all(psi_copies)

    @pl.loop(0, sectors, unroll=2)
    def _(s):
        for h in range(2):
            inner[:, s, :, h * cols : (h + 1) * cols] = first_stage(left_ref, psi[h, s], inner.shape)

    wait_all(right_copies)
    acc = second_stage([inner.at[table_ref[i]] for i in early + late], right, cols)
    before = jnp.zeros((rows, cols), jnp.float32)
    after = jnp.zeros((rows, cols), jnp.float32)
    for s in range(sectors):
        old = prev_ref[s]
        moved = step_rows(old, acc, sizes_ref, scal_ref, factor_ref[0], s)
        low[s] = moved.astype(jnp.bfloat16)
        before += old * old
        after += moved * moved
    for i in range(local):
        keep_ref[i * rows : (i + 1) * rows] = low[sec * local + i]
        send_ref[i * rows : (i + 1) * rows] = low[(1 - sec) * local + i]
    keep_ref[local * rows : (local + 1) * rows] = low[0]
    send_ref[local * rows : (local + 1) * rows] = low[0]
    tail = keep_ref.shape[0] - (local + 1) * rows
    line = lax.broadcasted_iota(jnp.int32, (tail, cols), 0)
    stats = jnp.zeros((tail, cols), jnp.float32)
    for i, total in enumerate((before, after)):
        parts = split_3(jnp.full((tail, cols), jnp.sum(total), jnp.float32))
        for p, low_part in enumerate(parts):
            stats = jnp.where(line == 3 * i + p, low_part.astype(jnp.float32), stats)
    keep_ref[(local + 1) * rows :] = stats.astype(jnp.bfloat16)
    send_ref[(local + 1) * rows :] = stats.astype(jnp.bfloat16)


def final_kernel(slots, values, *refs):
    n_slots = len(slots)
    scal_ref, table_ref, weights_ref = refs[:3]
    left_refs = refs[3:6]
    pieces = refs[6 : 6 + 2 * n_slots]
    wave_ref, mixed_ref, basis, lefts, sems = refs[6 + 2 * n_slots :]
    copies = copy_in([(ref, lefts.at[d]) for d, ref in enumerate(left_refs)], sems)
    core, sec = scal_ref[1], scal_ref[2]
    local, width, _ = wave_ref.shape
    cols = width // 2
    rows = width // n_slots
    tail = pieces[0].shape[0] - (local + 1) * rows
    stats = jnp.zeros((tail, cols), jnp.float32)
    views = []
    for i, piece in enumerate(pieces):
        at = pl.ds(pl.multiple_of(table_ref[i % n_slots] * rows, rows), rows)
        side = sec if i < n_slots else 1 - sec
        across = pl.ds(pl.multiple_of(side * cols, cols), cols)
        views.append((piece, at, across))
        stats += piece[(local + 1) * rows :].astype(jnp.float32)
        basis[at, across] = piece[local * rows : (local + 1) * rows]
    line = lax.broadcasted_iota(jnp.int32, (tail, cols), 0)
    first = jnp.sum(jnp.where(line < 3, stats, 0.0), axis=0, keepdims=True)[:, :1]
    second = jnp.sum(jnp.where((line >= 3) & (line < 6), stats, 0.0), axis=0, keepdims=True)[:, :1]
    norm_1 = jnp.sqrt(first / values + 1e-06)
    norm_2 = jnp.sqrt(second / (norm_1 * norm_1) / values + 1e-06)
    scale = 1.0 / (norm_1 * norm_2)
    for s in range(local):
        for view, at, across in views:
            wave_ref[s, at, across] = view[s * rows : (s + 1) * rows].astype(jnp.float32) * scale
    across = pl.ds(pl.multiple_of(sec * cols, cols), cols)
    swapped = core != 0
    weights = (
        weights_ref[1],
        jnp.where(swapped, weights_ref[2], weights_ref[0]),
        jnp.where(swapped, weights_ref[0], weights_ref[2]),
    )
    wait_all(copies)
    mixer = sum(weights[d] * lefts[d].astype(jnp.float32) for d in range(3))
    right = jnp.dot(mixer.astype(jnp.bfloat16), basis[:, across], preferred_element_type=jnp.float32)
    rotated = lax.dot_general(
        basis[...], right.astype(jnp.bfloat16), (((0,), (0,)), ((), ())), preferred_element_type=jnp.float32
    )
    mixed_ref[...] = (rotated * (scale * scale / width)).astype(jnp.bfloat16)


def kernel_call(body, out, ins, scratch, mib, flops, moved):
    spaces = {"s": SMEM, "v": VMEM, "a": pl.ANY, "h": pltpu.MemorySpace.HBM}
    multiple = isinstance(out, (tuple, list))
    out_spec = pl.BlockSpec(memory_space=VMEM)
    return pl.pallas_call(
        body,
        out_shape=out,
        in_specs=[pl.BlockSpec(memory_space=spaces[c]) for c in ins],
        out_specs=(out_spec,) * len(out) if multiple else out_spec,
        scratch_shapes=scratch,
        compiler_params=pltpu.CompilerParams(vmem_limit_bytes=mib * 1024 * 1024),
        cost_estimate=pl.CostEstimate(flops=flops, bytes_accessed=moved, transcendentals=0),
    )


def gather_form(wavefunction, left_ops, right_ops, shift_map, sector_sizes, step_sizes, integrals):
    f32, bf16 = jnp.float32, jnp.bfloat16
    n = lax.axis_size("ops")
    local, width, _ = wavefunction.shape
    sectors = sector_sizes.shape[0]
    rows, cols = width // n, width // 2
    o, sec = lax.axis_index("ops"), lax.axis_index("sec")
    core = lax.rem(o, 2)
    slots = ring_slots(n)
    n_slots = len(slots)
    late = [n_slots // 2 - 1, n_slots - 1]
    early = [i for i in range(n_slots) if i not in late]
    scal = jnp.stack([o, core, sec]).astype(jnp.int32)
    table = lax.dynamic_slice_in_dim(jnp.asarray(ring_table(n)), o, 1, 0)[0]
    factors = step_sizes.astype(f32) / (8.0 * math.sqrt(n))
    shape = jax.ShapeDtypeStruct
    dma = pltpu.SemaphoreType.DMA
    psi_bytes = 2 * sectors * width**2
    tall = cols + 16

    right_cols = jnp.concatenate(
        [
            lax.dynamic_slice_in_dim(right_ops[0], sec * cols, cols, 0),
            jnp.broadcast_to(shift_map.astype(bf16)[:, None], (16, width)),
        ]
    )
    right_pieces = ring_gather(right_cols, n)
    left_rows = lax.all_to_all(left_ops[0], "ops", 0, 0, tiled=True)
    part = lax.dynamic_slice_in_dim(wavefunction, core * (local // 2), local // 2, 0)
    near = swap_sec(part)
    far = swap_core(near, n)

    inner = kernel_call(
        own_kernel, shape((n, local, rows, width), bf16), "ssva",
        [pltpu.VMEM((local, width, width), bf16), dma((local,))],
        10, sectors * width**3, psi_bytes,
    )(scal, sector_sizes, left_rows, wavefunction)
    acc, rest, right_early = kernel_call(
        functools.partial(early_kernel, early, late),
        (
            shape((sectors * rows, cols), f32),
            shape((2, sectors, rows, width), bf16),
            shape((len(early), tall, width), bf16),
        ),
        "sssvaaa" + "a" * len(early),
        [
            pltpu.VMEM((n, sectors, rows, width), bf16),
            pltpu.VMEM((local, width, width), bf16),
            dma((local,)),
            dma((len(early),)),
            dma((1,)),
        ],
        16, 2 * sectors * width**2 * cols, 2 * psi_bytes,
    )(scal, table, sector_sizes, left_rows, inner, near, far, *[right_pieces[i] for i in early])
    psi_1, low_1 = kernel_call(
        late_kernel,
        (shape((sectors, rows, cols), f32), shape((sectors, rows, cols), bf16)),
        "sssvvaaaaa",
        [pltpu.VMEM((2, tall, width), bf16), pltpu.VMEM((sectors, rows, cols), bf16), dma((2,)), dma((3,))],
        8, sectors * width * cols * cols, psi_bytes // 4,
    )(scal, sector_sizes, factors[:1], acc, rest, wavefunction, near, far, *[right_pieces[i] for i in late])

    low_2 = swap_sec(low_1)
    pairs = [(k, k + 1) for k in range(1, n - 1, 2)]
    left_cross = lax.ppermute(left_ops[0], "ops", pairs + [(b, a) for a, b in pairs])
    left_local = swap_core(left_ops[0], n)
    psi_pieces = ring_gather(low_1, n) + ring_gather(low_2, n)
    message = (local + 1) * rows + 16
    keep, send = kernel_call(
        functools.partial(iter2_kernel, n_slots, early, late), (shape((message, cols), bf16),) * 2,
        "ssssvv" + "a" * (2 * n_slots + 3),
        [
            pltpu.VMEM((2, sectors, width, cols), bf16),
            pltpu.VMEM((n, sectors, rows, width), bf16),
            pltpu.VMEM((n, tall, width), bf16),
            pltpu.VMEM((sectors, rows, cols), bf16),
            dma((2 * n_slots,)),
            dma((3,)),
        ],
        18, 3 * sectors * width**3, 2 * psi_bytes,
    )(scal, table, sector_sizes, factors[1:2], left_rows, psi_1, *psi_pieces, right_early, *[right_pieces[i] for i in late])

    recv = swap_sec(send)
    last_pieces = ring_gather(keep, n) + ring_gather(recv, n)
    wave, mixed = kernel_call(
        functools.partial(final_kernel, slots, float(sectors * width * width)),
        (shape((local, width, width), f32), shape((width, cols), bf16)),
        "sssaaa" + "v" * (2 * n_slots),
        [pltpu.VMEM((width, width), bf16), pltpu.VMEM((3, width, width), bf16), dma((3,))],
        16, 2 * width**3, 6 * local * width**2,
    )(scal, table, integrals[0], left_ops[0], left_cross, left_local, *last_pieces)
    return (wave, mixed[None])


def shards(wavefunction, left_ops, right_ops, *rest):
    n, halves = lax.axis_size("ops"), lax.axis_size("sec")
    width = right_ops.shape[1]
    gathered = 2 * n * right_ops.size // halves
    fits = gathered <= GATHER_BYTES and halves == 2 and right_ops.shape[0] == 1
    aligned = n % 4 == 0 and width % (16 * n) == 0 and width % 256 == 0 and wavefunction.shape[0] % 2 == 0
    form = gather_form if fits and aligned else reduce_form
    return form(wavefunction, left_ops, right_ops, *rest)


def solution(mesh):
    placed = (
        P("sec", None, None),
        P("ops", None, None),
        P("ops", None, None),
        P("ops"),
        P(),
        P(),
        P("ops", None),
    )
    return jax.shard_map(
        shards,
        mesh=mesh,
        in_specs=placed,
        out_specs=(P("sec", None, None), P("ops", None, "sec")),
        check_vma=False,
    )
```

```python
import functools
import math

import jax
import jax.numpy as jnp
import numpy as np
from jax import lax
from jax.experimental import pallas as pl
from jax.experimental.pallas import tpu as pltpu
from jax.sharding import PartitionSpec as P


ITERS = 2
GATHER_BYTES = 8 * 1024 * 1024
VMEM = pltpu.MemorySpace.VMEM
SMEM = pltpu.MemorySpace.SMEM


def broadcast(value, axis, source):
    kept = jnp.where(lax.axis_index(axis) == source, value, 0).astype(value.dtype)
    return lax.psum(kept, axis)


def padded_2(cells, sides, width):
    for axis, dim in sides:
        count = lax.axis_size(axis)
        ends = count - 1
        head = lax.slice_in_dim(cells, 0, width, axis=dim)
        tail = lax.slice_in_dim(cells, cells.shape[dim] - width, cells.shape[dim], axis=dim)
        cells = jnp.concatenate(
            [
                lax.ppermute(tail, axis, [(i, (i + 1) % count) for i in range(ends)]),
                cells,
                lax.ppermute(head, axis, [((i + 1) % count, i) for i in range(ends)]),
            ],
            axis=dim,
        )
    return cells


def reduce_form(wavefunction, left_ops, right_ops, shift_map, sector_sizes, step_sizes, integrals):
    highest = lax.Precision.HIGHEST
    local_sec = wavefunction.shape[0]
    width = wavefunction.shape[1]
    sectors = sector_sizes.shape[0]
    count = lax.axis_size("ops") * left_ops.shape[0]
    first = lax.axis_index("sec") * local_sec
    local_sizes = lax.dynamic_slice_in_dim(sector_sizes, first, local_sec, 0)
    column = jnp.arange(width, dtype=jnp.int32)
    row_ok = (column[None, :] < local_sizes[:, None]).astype(jnp.float32)
    mask = row_ok[:, :, None] * row_ok[:, None, :]
    psi = wavefunction.astype(jnp.float32) * mask
    sources = first + jnp.arange(local_sec, dtype=jnp.int32)
    target = (sources[None, :] + shift_map[:, None]) % sectors
    routing = (jnp.arange(sectors, dtype=jnp.int32)[:, None, None] == target[None]).astype(
        jnp.float32
    )
    for step in range(ITERS):
        psi_low = psi.astype(jnp.bfloat16)
        inner = jnp.einsum(
            "kmn,snp->ksmp", left_ops, psi_low, preferred_element_type=jnp.float32
        ).astype(jnp.bfloat16)
        terms = jnp.einsum("ksmp,kqp->ksmq", inner, right_ops, preferred_element_type=jnp.float32)
        contrib = jnp.einsum("tks,ksmq->tmq", routing, terms, precision=highest)
        partial_rows = lax.psum_scatter(contrib, "ops", scatter_dimension=1, tiled=True)
        own_rows = lax.psum_scatter(
            partial_rows.astype(jnp.bfloat16), "sec", scatter_dimension=0, tiled=True
        ).astype(jnp.float32)
        hpsi = lax.all_gather(own_rows.astype(jnp.bfloat16), "ops", axis=1, tiled=True).astype(
            own_rows.dtype
        )
        factor = step_sizes[step].astype(jnp.float32) / (8.0 * math.sqrt(count))
        psi = mask * (psi - factor * hpsi)
        total = lax.psum(jnp.sum(psi * psi), "sec")
        psi = psi / jnp.sqrt(total / (sectors * width * width) + 1e-06)
    basis = broadcast(psi[0].astype(jnp.bfloat16), "sec", 0)
    col_count = width // lax.axis_size("sec")
    basis_cols = lax.dynamic_slice_in_dim(basis, lax.axis_index("sec") * col_count, col_count, 1)
    half = jnp.einsum("mp,kmn->kpn", basis, left_ops, preferred_element_type=jnp.float32).astype(
        jnp.bfloat16
    )
    rotated = (
        jnp.einsum("kpn,nq->kpq", half, basis_cols, preferred_element_type=jnp.float32) / width
    )
    padded = padded_2(rotated.astype(jnp.bfloat16), (("ops", 0),), 1).astype(rotated.dtype)
    mixed = (
        integrals[:, 0, None, None] * padded[:-2]
        + integrals[:, 1, None, None] * padded[1:-1]
        + integrals[:, 2, None, None] * padded[2:]
    )
    return (psi, mixed.astype(jnp.bfloat16))


def ring_order(chips):
    return list(range(0, chips, 2)) + list(range(chips - 1, 0, -2))


def swap_core(x, n):
    return lax.ppermute(x, "ops", [(o, o ^ 1) for o in range(n)])


def swap_sec(x):
    return lax.ppermute(x, "sec", [(0, 1), (1, 0)])


def along_ring(x, n, by):
    order = ring_order(n // 2)
    place = {chip: i for i, chip in enumerate(order)}
    perm = []
    for o in range(n):
        chip = order[(place[o // 2] + by) % len(order)]
        perm.append((o, 2 * chip + o % 2))
    return lax.ppermute(x, "ops", perm)


def ring_slots(n):
    slots = [(0, 0)]
    for step in range(1, n // 4):
        slots += [(-step, 0), (step, 0)]
    slots.append((-(n // 4), 0))
    return slots + [(d, 1) for d, _ in slots]


def ring_table(n):
    order = ring_order(n // 2)
    place = {chip: i for i, chip in enumerate(order)}
    rows = []
    for o in range(n):
        at = place[o // 2]
        rows.append([2 * order[(at + d) % len(order)] + ((o % 2) ^ c) for d, c in ring_slots(n)])
    return np.array(rows, np.int32)


def ring_gather(x, n):
    last = n // 4
    up = down = x
    own = [x]
    for step in range(1, last + 1):
        up = along_ring(up, n, 1)
        own.append(up)
        if step < last:
            down = along_ring(down, n, -1)
            own.append(down)
    other = []
    for piece in own:
        other.append(swap_core(piece, n))
    return own + other


def copy_in(pairs, sems):
    copies = []
    for i, (src, dst) in enumerate(pairs):
        copy = pltpu.make_async_copy(src, dst, sems.at[i])
        copy.start()
        copies.append(copy)
    return copies


def wait_all(copies):
    for copy in copies:
        copy.wait()


def cut_psi(psi, size):
    row = lax.broadcasted_iota(jnp.int32, (psi.shape[0], 1), 0)
    col = lax.broadcasted_iota(jnp.int32, (1, psi.shape[1]), 1)
    rows = jnp.where(row < size, 1.0, 0.0).astype(psi.dtype)
    cols = jnp.where(col < size, 1.0, 0.0).astype(psi.dtype)
    return psi * rows * cols


def first_stage(left_ref, psi, inner_shape):
    product = jnp.dot(left_ref[...], psi, preferred_element_type=jnp.float32).astype(jnp.bfloat16)
    return product.reshape(inner_shape[0], inner_shape[2], psi.shape[1])


def own_kernel(scal_ref, sizes_ref, mine_ref, other_ref, wave_ref, out_ref, left_ref, waves, sems):
    local = wave_ref.shape[0]
    copies = copy_in([(wave_ref.at[i], waves.at[i]) for i in range(local)], sems)
    sec, cols = scal_ref[2], mine_ref.shape[1]
    left_ref[:, pl.ds(pl.multiple_of(sec * cols, cols), cols)] = mine_ref[...]
    left_ref[:, pl.ds(pl.multiple_of((1 - sec) * cols, cols), cols)] = other_ref[...]
    for i in range(local):
        copies[i].wait()
        psi = cut_psi(waves[i], sizes_ref[scal_ref[2] * local + i])
        out_ref[:, i] = first_stage(left_ref, psi, out_ref.shape)


def second_stage(terms, right, cols):
    total = None
    for i, inner in enumerate(terms):
        sectors, _, _ = inner.shape
        shift = jnp.max(right[i, cols:, :128].astype(jnp.float32)).astype(jnp.int32)
        rhs = right[i, :cols]
        lhs = jnp.concatenate([inner[lax.rem(t - shift + sectors, sectors)] for t in range(sectors)], axis=0)
        product = lax.dot_general(
            lhs, rhs, (((1,), (1,)), ((), ())), preferred_element_type=jnp.float32
        )
        total = product if total is None else total + product
    return total


def step_rows(psi, acc, sizes_ref, scal_ref, factor, sector):
    rows, cols = psi.shape
    size = sizes_ref[sector]
    row = lax.broadcasted_iota(jnp.int32, psi.shape, 0) + scal_ref[0] * rows
    col = lax.broadcasted_iota(jnp.int32, psi.shape, 1) + scal_ref[2] * cols
    moved = psi - factor * acc[sector * rows : (sector + 1) * rows]
    return jnp.where((row < size) & (col < size), moved, 0.0)


def early_kernel(early, late, *refs):
    scal_ref, table_ref, sizes_ref, left_ref, own_ref = refs[:5]
    local = own_ref.shape[1]
    half = local // 2
    sources = refs[5:7]
    pieces = refs[7 : 7 + len(early)]
    acc_ref, rest_ref, right, inner, waves, wsems, rsems, isem = refs[7 + len(early) :]
    core, sec = scal_ref[1], scal_ref[2]
    cols = acc_ref.shape[1]
    wave_copies = copy_in(
        [(ref.at[i], waves.at[c * half + i]) for c, ref in enumerate(sources) for i in range(half)], wsems
    )
    copies = copy_in([(own_ref, inner.at[:, pl.ds(sec * local, local)])], isem)
    copies += copy_in([(piece, right.at[i]) for i, piece in enumerate(pieces)], rsems)
    foreign = (1 - sec) * local
    swapped = core * half

    for slot in range(local):
        wave_copies[slot].wait()
        sector = foreign + lax.rem(swapped + slot, local)
        psi = cut_psi(waves[slot], sizes_ref[sector])
        inner[:, sector] = first_stage(left_ref, psi, inner.shape)

    wait_all(copies)
    acc_ref[...] = second_stage([inner.at[table_ref[i]] for i in early], right, cols)
    for at, i in enumerate(late):
        rest_ref[at] = inner[table_ref[i]]


def late_kernel(*refs):
    scal_ref, sizes_ref, factor_ref, acc_ref, rest_ref, own_ref = refs[:6]
    local = own_ref.shape[0]
    others = refs[6:8]
    pieces = refs[8:10]
    out_ref, send_ref, right, start, rsems, ssems = refs[10:]
    o, core, sec = scal_ref[0], scal_ref[1], scal_ref[2]
    _, rows, cols = out_ref.shape
    here = (slice(None), pl.ds(o * rows, rows), pl.ds(sec * cols, cols))
    foreign, half = (1 - sec) * local, local // 2
    copies = copy_in([(piece, right.at[c]) for c, piece in enumerate(pieces)], rsems)
    moves = [(own_ref.at[here], start.at[pl.ds(sec * local, local)])]
    for c, ref in enumerate(others):
        moves.append((ref.at[here], start.at[pl.ds(foreign + lax.rem((core + c) * half, local), half)]))
    copies += copy_in(moves, ssems)
    wait_all(copies)
    acc = acc_ref[...] + second_stage([rest_ref.at[c] for c in range(2)], right, cols)
    for s in range(out_ref.shape[0]):
        moved = step_rows(start[s].astype(jnp.float32), acc, sizes_ref, scal_ref, factor_ref[0], s)
        out_ref[s] = moved
        send_ref[s] = moved.astype(jnp.bfloat16)


def split_3(value):
    parts = []
    for _ in range(3):
        low = value.astype(jnp.bfloat16)
        parts.append(low)
        value = value - low.astype(jnp.float32)
    return parts


def iter2_kernel(n_slots, early, late, *refs):
    scal_ref, table_ref, sizes_ref, factor_ref, left_ref, prev_ref = refs[:6]
    psi_pieces = refs[6 : 6 + 2 * n_slots]
    right_pieces = refs[6 + 2 * n_slots : 9 + 2 * n_slots]
    keep_ref, send_ref, psi, inner, right, low, psems, rsems = refs[9 + 2 * n_slots :]
    sec = scal_ref[2]
    sectors, rows, cols = prev_ref.shape
    local = sectors // 2
    pairs = []
    for i, piece in enumerate(psi_pieces):
        at = pl.ds(table_ref[i % n_slots] * rows, rows)
        pairs.append((piece, psi.at[sec if i < n_slots else 1 - sec, :, at]))
    psi_copies = copy_in(pairs, psems)
    right_copies = copy_in(
        [(right_pieces[0], right.at[pl.ds(0, len(early))])]
        + [(right_pieces[1 + c], right.at[len(early) + c]) for c in range(2)],
        rsems,
    )
    wait_all(psi_copies)

    @pl.loop(0, sectors, unroll=2)
    def _(s):
        for h in range(2):
            inner[:, s, :, h * cols : (h + 1) * cols] = first_stage(left_ref, psi[h, s], inner.shape)

    wait_all(right_copies)
    acc = second_stage([inner.at[table_ref[i]] for i in early + late], right, cols)
    before = jnp.zeros((rows, cols), jnp.float32)
    after = jnp.zeros((rows, cols), jnp.float32)
    for s in range(sectors):
        old = prev_ref[s]
        moved = step_rows(old, acc, sizes_ref, scal_ref, factor_ref[0], s)
        low[s] = moved.astype(jnp.bfloat16)
        before += old * old
        after += moved * moved
    for i in range(local):
        keep_ref[i * rows : (i + 1) * rows] = low[sec * local + i]
        send_ref[i * rows : (i + 1) * rows] = low[(1 - sec) * local + i]
    keep_ref[local * rows : (local + 1) * rows] = low[0]
    send_ref[local * rows : (local + 1) * rows] = low[0]
    tail = keep_ref.shape[0] - (local + 1) * rows
    line = lax.broadcasted_iota(jnp.int32, (tail, cols), 0)
    stats = jnp.zeros((tail, cols), jnp.float32)
    for i, total in enumerate((before, after)):
        parts = split_3(jnp.full((tail, cols), jnp.sum(total), jnp.float32))
        for p, low_part in enumerate(parts):
            stats = jnp.where(line == 3 * i + p, low_part.astype(jnp.float32), stats)
    keep_ref[(local + 1) * rows :] = stats.astype(jnp.bfloat16)
    send_ref[(local + 1) * rows :] = stats.astype(jnp.bfloat16)


def final_kernel(slots, values, *refs):
    n_slots = len(slots)
    scal_ref, table_ref, weights_ref = refs[:3]
    left_refs = refs[3:6]
    pieces = refs[6 : 6 + 2 * n_slots]
    wave_ref, mixed_ref, basis, lefts, sems = refs[6 + 2 * n_slots :]
    copies = copy_in([(ref, lefts.at[d]) for d, ref in enumerate(left_refs)], sems)
    core, sec = scal_ref[1], scal_ref[2]
    local, width, _ = wave_ref.shape
    cols = width // 2
    rows = width // n_slots
    tail = pieces[0].shape[0] - (local + 1) * rows
    stats = jnp.zeros((tail, cols), jnp.float32)
    views = []
    for i, piece in enumerate(pieces):
        at = pl.ds(pl.multiple_of(table_ref[i % n_slots] * rows, rows), rows)
        side = sec if i < n_slots else 1 - sec
        across = pl.ds(pl.multiple_of(side * cols, cols), cols)
        views.append((piece, at, across))
        stats += piece[(local + 1) * rows :].astype(jnp.float32)
        basis[at, across] = piece[local * rows : (local + 1) * rows]
    line = lax.broadcasted_iota(jnp.int32, (tail, cols), 0)
    first = jnp.sum(jnp.where(line < 3, stats, 0.0), axis=0, keepdims=True)[:, :1]
    second = jnp.sum(jnp.where((line >= 3) & (line < 6), stats, 0.0), axis=0, keepdims=True)[:, :1]
    norm_1 = jnp.sqrt(first / values + 1e-06)
    norm_2 = jnp.sqrt(second / (norm_1 * norm_1) / values + 1e-06)
    scale = 1.0 / (norm_1 * norm_2)
    for s in range(local):
        for view, at, across in views:
            wave_ref[s, at, across] = view[s * rows : (s + 1) * rows].astype(jnp.float32) * scale
    across = pl.ds(pl.multiple_of(sec * cols, cols), cols)
    swapped = core != 0
    weights = (
        weights_ref[1],
        jnp.where(swapped, weights_ref[2], weights_ref[0]),
        jnp.where(swapped, weights_ref[0], weights_ref[2]),
    )
    wait_all(copies)
    mixer = sum(weights[d] * lefts[d].astype(jnp.float32) for d in range(3))
    right = jnp.dot(mixer.astype(jnp.bfloat16), basis[:, across], preferred_element_type=jnp.float32)
    rotated = lax.dot_general(
        basis[...], right.astype(jnp.bfloat16), (((0,), (0,)), ((), ())), preferred_element_type=jnp.float32
    )
    mixed_ref[...] = (rotated * (scale * scale / width)).astype(jnp.bfloat16)


def kernel_call(body, out, ins, scratch, mib, flops, moved):
    spaces = {"s": SMEM, "v": VMEM, "a": pl.ANY, "h": pltpu.MemorySpace.HBM}
    multiple = isinstance(out, (tuple, list))
    out_spec = pl.BlockSpec(memory_space=VMEM)
    return pl.pallas_call(
        body,
        out_shape=out,
        in_specs=[pl.BlockSpec(memory_space=spaces[c]) for c in ins],
        out_specs=(out_spec,) * len(out) if multiple else out_spec,
        scratch_shapes=scratch,
        compiler_params=pltpu.CompilerParams(vmem_limit_bytes=mib * 1024 * 1024),
        cost_estimate=pl.CostEstimate(flops=flops, bytes_accessed=moved, transcendentals=0),
    )


def gather_form(wavefunction, left_ops, right_ops, shift_map, sector_sizes, step_sizes, integrals):
    f32, bf16 = jnp.float32, jnp.bfloat16
    n = lax.axis_size("ops")
    local, width, _ = wavefunction.shape
    sectors = sector_sizes.shape[0]
    rows, cols = width // n, width // 2
    o, sec = lax.axis_index("ops"), lax.axis_index("sec")
    core = lax.rem(o, 2)
    slots = ring_slots(n)
    n_slots = len(slots)
    late = [n_slots // 2 - 1, n_slots - 1]
    early = [i for i in range(n_slots) if i not in late]
    scal = jnp.stack([o, core, sec]).astype(jnp.int32)
    table = lax.dynamic_slice_in_dim(jnp.asarray(ring_table(n)), o, 1, 0)[0]
    factors = step_sizes.astype(f32) / (8.0 * math.sqrt(n))
    shape = jax.ShapeDtypeStruct
    dma = pltpu.SemaphoreType.DMA
    psi_bytes = 2 * sectors * width**2
    tall = cols + 16

    right_cols = jnp.concatenate(
        [
            lax.dynamic_slice_in_dim(right_ops[0], sec * cols, cols, 0),
            jnp.broadcast_to(shift_map.astype(bf16)[:, None], (16, width)),
        ]
    )
    right_pieces = ring_gather(right_cols, n)
    near = swap_sec(lax.dynamic_slice_in_dim(wavefunction, core * (local // 2), local // 2, 0))
    far = swap_core(near, n)
    left_mine = lax.all_to_all(lax.dynamic_slice_in_dim(left_ops[0], sec * cols, cols, 1), "ops", 0, 0, tiled=True)
    left_other = swap_sec(left_mine)

    inner, left_rows = kernel_call(
        own_kernel, (shape((n, local, rows, width), bf16), shape((width, width), bf16)), "ssvva",
        [pltpu.VMEM((local, width, width), bf16), dma((local,))],
        10, sectors * width**3, psi_bytes,
    )(scal, sector_sizes, left_mine, left_other, wavefunction)
    acc, rest, right_early = kernel_call(
        functools.partial(early_kernel, early, late),
        (
            shape((sectors * rows, cols), f32),
            shape((2, sectors, rows, width), bf16),
            shape((len(early), tall, width), bf16),
        ),
        "sssvaaa" + "a" * len(early),
        [
            pltpu.VMEM((n, sectors, rows, width), bf16),
            pltpu.VMEM((local, width, width), bf16),
            dma((local,)),
            dma((len(early),)),
            dma((1,)),
        ],
        16, 2 * sectors * width**2 * cols, 2 * psi_bytes,
    )(scal, table, sector_sizes, left_rows, inner, near, far, *[right_pieces[i] for i in early])
    psi_1, low_1 = kernel_call(
        late_kernel,
        (shape((sectors, rows, cols), f32), shape((sectors, rows, cols), bf16)),
        "sssvvaaaaa",
        [pltpu.VMEM((2, tall, width), bf16), pltpu.VMEM((sectors, rows, cols), bf16), dma((2,)), dma((3,))],
        8, sectors * width * cols * cols, psi_bytes // 4,
    )(scal, sector_sizes, factors[:1], acc, rest, wavefunction, near, far, *[right_pieces[i] for i in late])

    low_2 = swap_sec(low_1)
    pairs = [(k, k + 1) for k in range(1, n - 1, 2)]
    left_cross = lax.ppermute(left_ops[0], "ops", pairs + [(b, a) for a, b in pairs])
    left_local = swap_core(left_ops[0], n)
    psi_pieces = ring_gather(low_1, n) + ring_gather(low_2, n)
    message = (local + 1) * rows + 16
    keep, send = kernel_call(
        functools.partial(iter2_kernel, n_slots, early, late), (shape((message, cols), bf16),) * 2,
        "ssssvv" + "a" * (2 * n_slots + 3),
        [
            pltpu.VMEM((2, sectors, width, cols), bf16),
            pltpu.VMEM((n, sectors, rows, width), bf16),
            pltpu.VMEM((n, tall, width), bf16),
            pltpu.VMEM((sectors, rows, cols), bf16),
            dma((2 * n_slots,)),
            dma((3,)),
        ],
        18, 3 * sectors * width**3, 2 * psi_bytes,
    )(scal, table, sector_sizes, factors[1:2], left_rows, psi_1, *psi_pieces, right_early, *[right_pieces[i] for i in late])

    recv = swap_sec(send)
    last_pieces = ring_gather(keep, n) + ring_gather(recv, n)
    wave, mixed = kernel_call(
        functools.partial(final_kernel, slots, float(sectors * width * width)),
        (shape((local, width, width), f32), shape((width, cols), bf16)),
        "sssaaa" + "v" * (2 * n_slots),
        [pltpu.VMEM((width, width), bf16), pltpu.VMEM((3, width, width), bf16), dma((3,))],
        16, 2 * width**3, 6 * local * width**2,
    )(scal, table, integrals[0], left_ops[0], left_cross, left_local, *last_pieces)
    return (wave, mixed[None])


def shards(wavefunction, left_ops, right_ops, *rest):
    n, halves = lax.axis_size("ops"), lax.axis_size("sec")
    width = right_ops.shape[1]
    gathered = 2 * n * right_ops.size // halves
    fits = gathered <= GATHER_BYTES and halves == 2 and right_ops.shape[0] == 1
    aligned = n % 4 == 0 and width % (16 * n) == 0 and width % 256 == 0 and wavefunction.shape[0] % 2 == 0
    form = gather_form if fits and aligned else reduce_form
    return form(wavefunction, left_ops, right_ops, *rest)


def solution(mesh):
    placed = (
        P("sec", None, None),
        P("ops", None, None),
        P("ops", None, None),
        P("ops"),
        P(),
        P(),
        P("ops", None),
    )
    return jax.shard_map(
        shards,
        mesh=mesh,
        in_specs=placed,
        out_specs=(P("sec", None, None), P("ops", None, "sec")),
        check_vma=False,
    )
```

```python
import functools
import math

import jax
import jax.numpy as jnp
import numpy as np
from jax import lax
from jax.experimental import pallas as pl
from jax.experimental.pallas import tpu as pltpu
from jax.sharding import PartitionSpec as P


ITERS = 2
GATHER_BYTES = 8 * 1024 * 1024
VMEM = pltpu.MemorySpace.VMEM
SMEM = pltpu.MemorySpace.SMEM


def broadcast(value, axis, source):
    kept = jnp.where(lax.axis_index(axis) == source, value, 0).astype(value.dtype)
    return lax.psum(kept, axis)


def padded_2(cells, sides, width):
    for axis, dim in sides:
        count = lax.axis_size(axis)
        ends = count - 1
        head = lax.slice_in_dim(cells, 0, width, axis=dim)
        tail = lax.slice_in_dim(cells, cells.shape[dim] - width, cells.shape[dim], axis=dim)
        cells = jnp.concatenate(
            [
                lax.ppermute(tail, axis, [(i, (i + 1) % count) for i in range(ends)]),
                cells,
                lax.ppermute(head, axis, [((i + 1) % count, i) for i in range(ends)]),
            ],
            axis=dim,
        )
    return cells


def reduce_form(wavefunction, left_ops, right_ops, shift_map, sector_sizes, step_sizes, integrals):
    highest = lax.Precision.HIGHEST
    local_sec = wavefunction.shape[0]
    width = wavefunction.shape[1]
    sectors = sector_sizes.shape[0]
    count = lax.axis_size("ops") * left_ops.shape[0]
    first = lax.axis_index("sec") * local_sec
    local_sizes = lax.dynamic_slice_in_dim(sector_sizes, first, local_sec, 0)
    column = jnp.arange(width, dtype=jnp.int32)
    row_ok = (column[None, :] < local_sizes[:, None]).astype(jnp.float32)
    mask = row_ok[:, :, None] * row_ok[:, None, :]
    psi = wavefunction.astype(jnp.float32) * mask
    sources = first + jnp.arange(local_sec, dtype=jnp.int32)
    target = (sources[None, :] + shift_map[:, None]) % sectors
    routing = (jnp.arange(sectors, dtype=jnp.int32)[:, None, None] == target[None]).astype(
        jnp.float32
    )
    for step in range(ITERS):
        psi_low = psi.astype(jnp.bfloat16)
        inner = jnp.einsum(
            "kmn,snp->ksmp", left_ops, psi_low, preferred_element_type=jnp.float32
        ).astype(jnp.bfloat16)
        terms = jnp.einsum("ksmp,kqp->ksmq", inner, right_ops, preferred_element_type=jnp.float32)
        contrib = jnp.einsum("tks,ksmq->tmq", routing, terms, precision=highest)
        partial_rows = lax.psum_scatter(contrib, "ops", scatter_dimension=1, tiled=True)
        own_rows = lax.psum_scatter(
            partial_rows.astype(jnp.bfloat16), "sec", scatter_dimension=0, tiled=True
        ).astype(jnp.float32)
        hpsi = lax.all_gather(own_rows.astype(jnp.bfloat16), "ops", axis=1, tiled=True).astype(
            own_rows.dtype
        )
        factor = step_sizes[step].astype(jnp.float32) / (8.0 * math.sqrt(count))
        psi = mask * (psi - factor * hpsi)
        total = lax.psum(jnp.sum(psi * psi), "sec")
        psi = psi / jnp.sqrt(total / (sectors * width * width) + 1e-06)
    basis = broadcast(psi[0].astype(jnp.bfloat16), "sec", 0)
    col_count = width // lax.axis_size("sec")
    basis_cols = lax.dynamic_slice_in_dim(basis, lax.axis_index("sec") * col_count, col_count, 1)
    half = jnp.einsum("mp,kmn->kpn", basis, left_ops, preferred_element_type=jnp.float32).astype(
        jnp.bfloat16
    )
    rotated = (
        jnp.einsum("kpn,nq->kpq", half, basis_cols, preferred_element_type=jnp.float32) / width
    )
    padded = padded_2(rotated.astype(jnp.bfloat16), (("ops", 0),), 1).astype(rotated.dtype)
    mixed = (
        integrals[:, 0, None, None] * padded[:-2]
        + integrals[:, 1, None, None] * padded[1:-1]
        + integrals[:, 2, None, None] * padded[2:]
    )
    return (psi, mixed.astype(jnp.bfloat16))


def ring_order(chips):
    return list(range(0, chips, 2)) + list(range(chips - 1, 0, -2))


def swap_core(x, n):
    return lax.ppermute(x, "ops", [(o, o ^ 1) for o in range(n)])


def swap_sec(x):
    return lax.ppermute(x, "sec", [(0, 1), (1, 0)])


def along_ring(x, n, by):
    order = ring_order(n // 2)
    place = {chip: i for i, chip in enumerate(order)}
    perm = []
    for o in range(n):
        chip = order[(place[o // 2] + by) % len(order)]
        perm.append((o, 2 * chip + o % 2))
    return lax.ppermute(x, "ops", perm)


def ring_slots(n):
    slots = [(0, 0)]
    for step in range(1, n // 4):
        slots += [(-step, 0), (step, 0)]
    slots.append((-(n // 4), 0))
    return slots + [(d, 1) for d, _ in slots]


def ring_table(n):
    order = ring_order(n // 2)
    place = {chip: i for i, chip in enumerate(order)}
    rows = []
    for o in range(n):
        at = place[o // 2]
        rows.append([2 * order[(at + d) % len(order)] + ((o % 2) ^ c) for d, c in ring_slots(n)])
    return np.array(rows, np.int32)


def ring_gather(x, n):
    last = n // 4
    up = down = x
    own = [x]
    for step in range(1, last + 1):
        up = along_ring(up, n, 1)
        own.append(up)
        if step < last:
            down = along_ring(down, n, -1)
            own.append(down)
    other = []
    for piece in own:
        other.append(swap_core(piece, n))
    return own + other


def copy_in(pairs, sems):
    copies = []
    for i, (src, dst) in enumerate(pairs):
        copy = pltpu.make_async_copy(src, dst, sems.at[i])
        copy.start()
        copies.append(copy)
    return copies


def wait_all(copies):
    for copy in copies:
        copy.wait()


def cut_psi(psi, size):
    row = lax.broadcasted_iota(jnp.int32, (psi.shape[0], 1), 0)
    col = lax.broadcasted_iota(jnp.int32, (1, psi.shape[1]), 1)
    rows = jnp.where(row < size, 1.0, 0.0).astype(psi.dtype)
    cols = jnp.where(col < size, 1.0, 0.0).astype(psi.dtype)
    return psi * rows * cols


def first_stage(left_ref, psi, inner_shape):
    product = jnp.dot(left_ref[...], psi, preferred_element_type=jnp.float32).astype(jnp.bfloat16)
    return product.reshape(inner_shape[0], inner_shape[2], psi.shape[1])


def own_kernel(scal_ref, sizes_ref, mine_ref, other_ref, wave_ref, out_ref, left_ref, waves, sems):
    local = wave_ref.shape[0]
    copies = copy_in([(wave_ref.at[i], waves.at[i]) for i in range(local)], sems)
    sec, cols = scal_ref[2], mine_ref.shape[1]
    left_ref[:, pl.ds(pl.multiple_of(sec * cols, cols), cols)] = mine_ref[...]
    left_ref[:, pl.ds(pl.multiple_of((1 - sec) * cols, cols), cols)] = other_ref[...]
    for i in range(local):
        copies[i].wait()
        psi = cut_psi(waves[i], sizes_ref[scal_ref[2] * local + i])
        out_ref[:, i] = first_stage(left_ref, psi, out_ref.shape)


def second_stage(terms, right, cols):
    total = None
    for i, inner in enumerate(terms):
        sectors, _, _ = inner.shape
        shift = jnp.max(right[i][cols:, :128].astype(jnp.float32)).astype(jnp.int32)
        rhs = right[i][:cols]
        lhs = jnp.concatenate([inner[lax.rem(t - shift + sectors, sectors)] for t in range(sectors)], axis=0)
        product = lax.dot_general(
            lhs, rhs, (((1,), (1,)), ((), ())), preferred_element_type=jnp.float32
        )
        total = product if total is None else total + product
    return total


def step_rows(psi, acc, sizes_ref, scal_ref, factor, sector):
    rows, cols = psi.shape
    size = sizes_ref[sector]
    row = lax.broadcasted_iota(jnp.int32, psi.shape, 0) + scal_ref[0] * rows
    col = lax.broadcasted_iota(jnp.int32, psi.shape, 1) + scal_ref[2] * cols
    moved = psi - factor * acc[sector * rows : (sector + 1) * rows]
    return jnp.where((row < size) & (col < size), moved, 0.0)


def early_kernel(early, late, *refs):
    scal_ref, table_ref, sizes_ref, left_ref, own_ref = refs[:5]
    local = own_ref.shape[1]
    half = local // 2
    sources = refs[5:7]
    pieces = refs[7 : 7 + len(early)]
    acc_ref, rest_ref, right, inner, waves, wsems, rsems, isem = refs[7 + len(early) :]
    core, sec = scal_ref[1], scal_ref[2]
    cols = acc_ref.shape[1]
    wave_copies = copy_in(
        [(ref.at[i], waves.at[c * half + i]) for c, ref in enumerate(sources) for i in range(half)], wsems
    )
    copies = copy_in([(own_ref, inner.at[:, pl.ds(sec * local, local)])], isem)
    copies += copy_in([(piece, right.at[i]) for i, piece in enumerate(pieces)], rsems)
    foreign = (1 - sec) * local
    swapped = core * half

    for slot in range(local):
        wave_copies[slot].wait()
        sector = foreign + lax.rem(swapped + slot, local)
        psi = cut_psi(waves[slot], sizes_ref[sector])
        inner[:, sector] = first_stage(left_ref, psi, inner.shape)

    wait_all(copies)
    places = [right.at[at] for at in range(len(early))]
    acc_ref[...] = second_stage([inner.at[table_ref[i]] for i in early], places, cols)
    for at, i in enumerate(late):
        rest_ref[at] = inner[table_ref[i]]


def late_kernel(*refs):
    scal_ref, sizes_ref, factor_ref, acc_ref, rest_ref, own_ref = refs[:6]
    local = own_ref.shape[0]
    others = refs[6:8]
    pieces = refs[8:10]
    out_ref, send_ref, right, start, rsems, ssems = refs[10:]
    o, core, sec = scal_ref[0], scal_ref[1], scal_ref[2]
    _, rows, cols = out_ref.shape
    here = (slice(None), pl.ds(o * rows, rows), pl.ds(sec * cols, cols))
    foreign, half = (1 - sec) * local, local // 2
    copies = copy_in([(piece, right.at[c]) for c, piece in enumerate(pieces)], rsems)
    moves = [(own_ref.at[here], start.at[pl.ds(sec * local, local)])]
    for c, ref in enumerate(others):
        moves.append((ref.at[here], start.at[pl.ds(foreign + lax.rem((core + c) * half, local), half)]))
    copies += copy_in(moves, ssems)
    wait_all(copies)
    acc = acc_ref[...] + second_stage([rest_ref.at[c] for c in range(2)], [right.at[c] for c in range(2)], cols)
    for s in range(out_ref.shape[0]):
        moved = step_rows(start[s].astype(jnp.float32), acc, sizes_ref, scal_ref, factor_ref[0], s)
        out_ref[s] = moved
        send_ref[s] = moved.astype(jnp.bfloat16)


def split_3(value):
    parts = []
    for _ in range(3):
        low = value.astype(jnp.bfloat16)
        parts.append(low)
        value = value - low.astype(jnp.float32)
    return parts


def iter2_kernel(n_slots, early, late, *refs):
    scal_ref, table_ref, sizes_ref, factor_ref, left_ref, prev_ref = refs[:6]
    psi_pieces = refs[6 : 6 + 2 * n_slots]
    right_pieces = refs[6 + 2 * n_slots : 9 + 2 * n_slots]
    keep_ref, send_ref, psi, inner, right, low, psems, rsems = refs[9 + 2 * n_slots :]
    sec = scal_ref[2]
    sectors, rows, cols = prev_ref.shape
    local = sectors // 2
    pairs = []
    for i, piece in enumerate(psi_pieces):
        at = pl.ds(table_ref[i % n_slots] * rows, rows)
        pairs.append((piece, psi.at[sec if i < n_slots else 1 - sec, :, at]))
    psi_copies = copy_in(pairs, psems)
    right_copies = copy_in([(right_pieces[1 + c], right.at[c]) for c in range(2)], rsems)
    wait_all(psi_copies)

    @pl.loop(0, sectors, unroll=4)
    def _(s):
        for h in range(2):
            inner[:, s, :, h * cols : (h + 1) * cols] = first_stage(left_ref, psi[h, s], inner.shape)

    wait_all(right_copies)
    places = [right_pieces[0].at[at] for at in range(len(early))] + [right.at[c] for c in range(2)]
    acc = second_stage([inner.at[table_ref[i]] for i in early + late], places, cols)
    before = jnp.zeros((rows, cols), jnp.float32)
    after = jnp.zeros((rows, cols), jnp.float32)
    for s in range(sectors):
        old = prev_ref[s]
        moved = step_rows(old, acc, sizes_ref, scal_ref, factor_ref[0], s)
        low[s] = moved.astype(jnp.bfloat16)
        before += old * old
        after += moved * moved
    for i in range(local):
        keep_ref[i * rows : (i + 1) * rows] = low[sec * local + i]
        send_ref[i * rows : (i + 1) * rows] = low[(1 - sec) * local + i]
    keep_ref[local * rows : (local + 1) * rows] = low[0]
    send_ref[local * rows : (local + 1) * rows] = low[0]
    tail = keep_ref.shape[0] - (local + 1) * rows
    line = lax.broadcasted_iota(jnp.int32, (tail, cols), 0)
    stats = jnp.zeros((tail, cols), jnp.float32)
    for i, total in enumerate((before, after)):
        parts = split_3(jnp.full((tail, cols), jnp.sum(total), jnp.float32))
        for p, low_part in enumerate(parts):
            stats = jnp.where(line == 3 * i + p, low_part.astype(jnp.float32), stats)
    keep_ref[(local + 1) * rows :] = stats.astype(jnp.bfloat16)
    send_ref[(local + 1) * rows :] = stats.astype(jnp.bfloat16)


def final_kernel(slots, values, *refs):
    n_slots = len(slots)
    scal_ref, table_ref, weights_ref = refs[:3]
    left_refs = refs[3:6]
    pieces = refs[6 : 6 + 2 * n_slots]
    wave_ref, mixed_ref, basis, lefts, sems = refs[6 + 2 * n_slots :]
    copies = copy_in([(ref, lefts.at[d]) for d, ref in enumerate(left_refs)], sems)
    core, sec = scal_ref[1], scal_ref[2]
    local, width, _ = wave_ref.shape
    cols = width // 2
    rows = width // n_slots
    tail = pieces[0].shape[0] - (local + 1) * rows
    stats = jnp.zeros((tail, cols), jnp.float32)
    views = []
    for i, piece in enumerate(pieces):
        at = pl.ds(pl.multiple_of(table_ref[i % n_slots] * rows, rows), rows)
        side = sec if i < n_slots else 1 - sec
        across = pl.ds(pl.multiple_of(side * cols, cols), cols)
        views.append((piece, at, across))
        stats += piece[(local + 1) * rows :].astype(jnp.float32)
        basis[at, across] = piece[local * rows : (local + 1) * rows]
    line = lax.broadcasted_iota(jnp.int32, (tail, cols), 0)
    first = jnp.sum(jnp.where(line < 3, stats, 0.0), axis=0, keepdims=True)[:, :1]
    second = jnp.sum(jnp.where((line >= 3) & (line < 6), stats, 0.0), axis=0, keepdims=True)[:, :1]
    norm_1 = jnp.sqrt(first / values + 1e-06)
    norm_2 = jnp.sqrt(second / (norm_1 * norm_1) / values + 1e-06)
    scale = 1.0 / (norm_1 * norm_2)
    for s in range(local):
        for view, at, across in views:
            wave_ref[s, at, across] = view[s * rows : (s + 1) * rows].astype(jnp.float32) * scale
    across = pl.ds(pl.multiple_of(sec * cols, cols), cols)
    swapped = core != 0
    weights = (
        weights_ref[1],
        jnp.where(swapped, weights_ref[2], weights_ref[0]),
        jnp.where(swapped, weights_ref[0], weights_ref[2]),
    )
    wait_all(copies)
    mixer = sum(weights[d] * lefts[d].astype(jnp.float32) for d in range(3))
    right = jnp.dot(mixer.astype(jnp.bfloat16), basis[:, across], preferred_element_type=jnp.float32)
    rotated = lax.dot_general(
        basis[...], right.astype(jnp.bfloat16), (((0,), (0,)), ((), ())), preferred_element_type=jnp.float32
    )
    mixed_ref[...] = (rotated * (scale * scale / width)).astype(jnp.bfloat16)


def kernel_call(body, out, ins, scratch, mib, flops, moved):
    spaces = {"s": SMEM, "v": VMEM, "a": pl.ANY, "h": pltpu.MemorySpace.HBM}
    multiple = isinstance(out, (tuple, list))
    out_spec = pl.BlockSpec(memory_space=VMEM)
    return pl.pallas_call(
        body,
        out_shape=out,
        in_specs=[pl.BlockSpec(memory_space=spaces[c]) for c in ins],
        out_specs=(out_spec,) * len(out) if multiple else out_spec,
        scratch_shapes=scratch,
        compiler_params=pltpu.CompilerParams(vmem_limit_bytes=mib * 1024 * 1024),
        cost_estimate=pl.CostEstimate(flops=flops, bytes_accessed=moved, transcendentals=0),
    )


def gather_form(wavefunction, left_ops, right_ops, shift_map, sector_sizes, step_sizes, integrals):
    f32, bf16 = jnp.float32, jnp.bfloat16
    n = lax.axis_size("ops")
    local, width, _ = wavefunction.shape
    sectors = sector_sizes.shape[0]
    rows, cols = width // n, width // 2
    o, sec = lax.axis_index("ops"), lax.axis_index("sec")
    core = lax.rem(o, 2)
    slots = ring_slots(n)
    n_slots = len(slots)
    late = [n_slots // 2 - 1, n_slots - 1]
    early = [i for i in range(n_slots) if i not in late]
    scal = jnp.stack([o, core, sec]).astype(jnp.int32)
    table = lax.dynamic_slice_in_dim(jnp.asarray(ring_table(n)), o, 1, 0)[0]
    factors = step_sizes.astype(f32) / (8.0 * math.sqrt(n))
    shape = jax.ShapeDtypeStruct
    dma = pltpu.SemaphoreType.DMA
    psi_bytes = 2 * sectors * width**2
    tall = cols + 16

    right_cols = jnp.concatenate(
        [
            lax.dynamic_slice_in_dim(right_ops[0], sec * cols, cols, 0),
            jnp.broadcast_to(shift_map.astype(bf16)[:, None], (16, width)),
        ]
    )
    right_pieces = ring_gather(right_cols, n)
    near = swap_sec(lax.dynamic_slice_in_dim(wavefunction, core * (local // 2), local // 2, 0))
    far = swap_core(near, n)
    left_mine = lax.all_to_all(lax.dynamic_slice_in_dim(left_ops[0], sec * cols, cols, 1), "ops", 0, 0, tiled=True)
    left_other = swap_sec(left_mine)

    inner, left_rows = kernel_call(
        own_kernel, (shape((n, local, rows, width), bf16), shape((width, width), bf16)), "ssvva",
        [pltpu.VMEM((local, width, width), bf16), dma((local,))],
        10, sectors * width**3, psi_bytes,
    )(scal, sector_sizes, left_mine, left_other, wavefunction)
    acc, rest, right_early = kernel_call(
        functools.partial(early_kernel, early, late),
        (
            shape((sectors * rows, cols), f32),
            shape((2, sectors, rows, width), bf16),
            shape((len(early), tall, width), bf16),
        ),
        "sssvaaa" + "a" * len(early),
        [
            pltpu.VMEM((n, sectors, rows, width), bf16),
            pltpu.VMEM((local, width, width), bf16),
            dma((local,)),
            dma((len(early),)),
            dma((1,)),
        ],
        16, 2 * sectors * width**2 * cols, 2 * psi_bytes,
    )(scal, table, sector_sizes, left_rows, inner, near, far, *[right_pieces[i] for i in early])
    psi_1, low_1 = kernel_call(
        late_kernel,
        (shape((sectors, rows, cols), f32), shape((sectors, rows, cols), bf16)),
        "sssvvaaaaa",
        [pltpu.VMEM((2, tall, width), bf16), pltpu.VMEM((sectors, rows, cols), bf16), dma((2,)), dma((3,))],
        8, sectors * width * cols * cols, psi_bytes // 4,
    )(scal, sector_sizes, factors[:1], acc, rest, wavefunction, near, far, *[right_pieces[i] for i in late])

    low_2 = swap_sec(low_1)
    pairs = [(k, k + 1) for k in range(1, n - 1, 2)]
    left_cross = lax.ppermute(left_ops[0], "ops", pairs + [(b, a) for a, b in pairs])
    left_local = swap_core(left_ops[0], n)
    psi_pieces = ring_gather(low_1, n) + ring_gather(low_2, n)
    message = (local + 1) * rows + 16
    keep, send = kernel_call(
        functools.partial(iter2_kernel, n_slots, early, late), (shape((message, cols), bf16),) * 2,
        "ssssvv" + "a" * (2 * n_slots) + "vaa",
        [
            pltpu.VMEM((2, sectors, width, cols), bf16),
            pltpu.VMEM((n, sectors, rows, width), bf16),
            pltpu.VMEM((2, tall, width), bf16),
            pltpu.VMEM((sectors, rows, cols), bf16),
            dma((2 * n_slots,)),
            dma((2,)),
        ],
        18, 3 * sectors * width**3, 2 * psi_bytes,
    )(scal, table, sector_sizes, factors[1:2], left_rows, psi_1, *psi_pieces, right_early, *[right_pieces[i] for i in late])

    recv = swap_sec(send)
    last_pieces = ring_gather(keep, n) + ring_gather(recv, n)
    wave, mixed = kernel_call(
        functools.partial(final_kernel, slots, float(sectors * width * width)),
        (shape((local, width, width), f32), shape((width, cols), bf16)),
        "sssaaa" + "v" * (2 * n_slots),
        [pltpu.VMEM((width, width), bf16), pltpu.VMEM((3, width, width), bf16), dma((3,))],
        16, 2 * width**3, 6 * local * width**2,
    )(scal, table, integrals[0], left_ops[0], left_cross, left_local, *last_pieces)
    return (wave, mixed[None])


def shards(wavefunction, left_ops, right_ops, *rest):
    n, halves = lax.axis_size("ops"), lax.axis_size("sec")
    width = right_ops.shape[1]
    gathered = 2 * n * right_ops.size // halves
    fits = gathered <= GATHER_BYTES and halves == 2 and right_ops.shape[0] == 1
    aligned = n % 4 == 0 and width % (16 * n) == 0 and width % 256 == 0 and wavefunction.shape[0] % 2 == 0
    form = gather_form if fits and aligned else reduce_form
    return form(wavefunction, left_ops, right_ops, *rest)


def solution(mesh):
    placed = (
        P("sec", None, None),
        P("ops", None, None),
        P("ops", None, None),
        P("ops"),
        P(),
        P(),
        P("ops", None),
    )
    return jax.shard_map(
        shards,
        mesh=mesh,
        in_specs=placed,
        out_specs=(P("sec", None, None), P("ops", None, "sec")),
        check_vma=False,
    )
```
